32 devices in a mesh: groups: 2 (over y), tr: 8 (over z, x), tc: 2 (over core).
Axes of the slice: x: 2, y: 2, z: 4, core: 2. Of those that a mesh axis runs over, the one named last changes fastest.
Arguments:
- shift_plane: float32 [2, 8192, 4096], P(None, ('groups', 'tr'), 'tc'), parts along dimension 1, may hold values from -0.2 to 0.2
- height: float32 [8192, 4096], P(('groups', 'tr'), 'tc'), parts along dimension 0, may hold values from -4 to 4
- dipole: float32 [8192, 4096], P(('groups', 'tr'), 'tc'), parts along dimension 0, may hold values from -6 to 6
Outputs:
- velocity_update: float32 [3, 8192, 4096], P(None, ('groups', 'tr'), 'tc'), parts along dimension 1
- dipole_update: float32 [8192, 4096], P(('groups', 'tr'), 'tc'), parts along dimension 0
The draws below stay inside these ranges and needn't reach their ends.
There are 2 independent parts, one for each index of `groups`. The reference program is written for one: setup_inputs(seed, part) draws one part's arguments, and reference() takes and returns one part's arrays. A program takes and returns all parts, laid end to end along the dimension named above; each array names one. Nothing has to cross between parts.
All inputs are finite; a program needn't handle non-finite values.
Results may differ from the reference program's by a relative error of at most 0.00009.
Values sent between devices are 32-bit elements; how exact they have to be, the bound alone decides.
A program may use at most 256 MiB of HBM per device.

```python
import jax
import jax.numpy as jnp

NB = 4096
NA = 4096


def block_scale(stream_key, dims, pieces, low, top_value):
    def one(position, blocks):
        draws = jax.random.uniform(jax.random.fold_in(jax.random.fold_in(stream_key, 6), position), (blocks,), jnp.float32, low / len(pieces), top_value / len(pieces))
        return jnp.repeat(jnp.exp(draws), dims[position] // blocks).reshape((-1,) + (1,) * (len(dims) - position - 1))

    gain = one(*pieces[0])
    for cut in pieces[1:]:
        gain = gain * one(*cut)
    return gain


def gaussian(rng, dims, width, limit, shards=(), kind=jnp.bfloat16):
    loudness = block_scale(rng, dims, shards, -0.22, 0.18) if shards else 1.0
    array = jax.random.normal(rng, dims, jnp.float32) * width * loudness
    return jnp.minimum(jnp.maximum(array, -limit), limit).astype(kind)


def setup_inputs(seed: int = 0, part: int = 0) -> dict:
    key_list = jax.random.split(jax.random.key(seed), 4)
    part_keys = jax.random.split(jax.random.fold_in(key_list[3], part), 4)
    shift_plane = jnp.clip(jax.random.uniform(part_keys[0], (2, NA, NB), jnp.float32, -0.2, 0.2) * block_scale(part_keys[0], (2, NA, NB), ((1, 8), (2, 2)), -0.4, 0.0), -0.2, 0.2)
    height = gaussian(part_keys[1], (NA, NB), 1.0, 4.0, ((0, 8), (1, 2)), jnp.float32)
    dipole = gaussian(part_keys[2], (NA, NB), 1.0, 6.0, ((0, 8), (1, 2)), jnp.float32)
    return {"shift_plane": shift_plane, "height": height, "dipole": dipole}


def first_diff(field, axis):
    return (jnp.roll(field, 2, axis) - 8.0 * jnp.roll(field, 1, axis) + 8.0 * jnp.roll(field, -1, axis) - jnp.roll(field, -2, axis)) / 12.0

def second_diff(field, axis):
    return (-jnp.roll(field, 2, axis) + 16.0 * jnp.roll(field, 1, axis) - 30.0 * field + 16.0 * jnp.roll(field, -1, axis) - jnp.roll(field, -2, axis)) / 12.0

def surface(grad_a, grad_b, curve_aa, curve_bb, curve_ab):
    tan_a = (1.0 + grad_a[0], grad_a[1], grad_a[2])
    tan_b = (grad_b[0], 1.0 + grad_b[1], grad_b[2])
    normal = (tan_a[1] * tan_b[2] - tan_a[2] * tan_b[1], tan_a[2] * tan_b[0] - tan_a[0] * tan_b[2], tan_a[0] * tan_b[1] - tan_a[1] * tan_b[0])
    area_stretch_factor = jnp.sqrt(normal[0] * normal[0] + normal[1] * normal[1] + normal[2] * normal[2])
    unit = (normal[0] / area_stretch_factor, normal[1] / area_stretch_factor, normal[2] / area_stretch_factor)
    first_edge_term = tan_a[0] * tan_a[0] + tan_a[1] * tan_a[1] + tan_a[2] * tan_a[2]
    first_f = tan_a[0] * tan_b[0] + tan_a[1] * tan_b[1] + tan_a[2] * tan_b[2]
    first_g = tan_b[0] * tan_b[0] + tan_b[1] * tan_b[1] + tan_b[2] * tan_b[2]
    second_l = curve_aa[0] * unit[0] + curve_aa[1] * unit[1] + curve_aa[2] * unit[2]
    second_m = curve_ab[0] * unit[0] + curve_ab[1] * unit[1] + curve_ab[2] * unit[2]
    second_n = curve_bb[0] * unit[0] + curve_bb[1] * unit[1] + curve_bb[2] * unit[2]
    curvature = (first_edge_term * second_n - 2.0 * first_f * second_m + first_g * second_l) / (2.0 * area_stretch_factor * area_stretch_factor)
    omega = (grad_a[3] / area_stretch_factor, grad_b[3] / area_stretch_factor)
    return (unit, curvature, omega)

def reference(shift_plane, height, dipole):
    fields = jnp.concatenate([shift_plane, height[None], dipole[None]], 0)
    grad_a = first_diff(fields, 1)
    grad_b = first_diff(fields, 2)
    curve_aa = second_diff(fields[:3], 1)
    curve_bb = second_diff(fields[:3], 2)
    curve_ab = first_diff(first_diff(fields[:3], 2), 1)
    unit, curvature, omega = surface(grad_a, grad_b, curve_aa, curve_bb, curve_ab)
    spec_one = jnp.fft.fft2(omega[0])
    spec_two = jnp.fft.fft2(omega[1])
    freq_one = jnp.fft.fftfreq(NA).astype(omega[0].dtype)[:, None]
    freq_two = jnp.fft.fftfreq(NB).astype(omega[0].dtype)[None, :]
    radius = jnp.sqrt(freq_one * freq_one + freq_two * freq_two)
    live = (jnp.abs(freq_one) < 0.5) & (jnp.abs(freq_two) < 0.5) & (radius > 0.0)
    factor = jnp.where(live, 0.5 / jnp.where(live, radius, 1.0), 0.0)
    summed = factor * (freq_one * spec_one + freq_two * spec_two)
    speed_hat = summed * -1j
    speed = jnp.real(jnp.fft.ifft2(speed_hat)).astype(height.dtype)
    velocity_update = jnp.stack([speed * unit[0], speed * unit[1], speed * unit[2]])
    dipole_update = -2.0 * 0.5 * 0.5 * height + 0.3 * curvature + 0.5 * speed * speed
    return (velocity_update.astype(jnp.float32), dipole_update.astype(jnp.float32))
```

```python
import math

import jax
import jax.numpy as jnp
import numpy as np
from jax import lax
from jax.experimental import pallas as pl
from jax.experimental.pallas import tpu as pltpu
from jax.sharding import PartitionSpec as P

largest_wavenumber = lax.Precision.HIGHEST


def padded_2(x, sides, width):
    for axis, dim in sides:
        devices, length = (lax.axis_size(axis), x.shape[dim])
        up = [(i, (i + 1) % devices) for i in range(devices)]
        down = [(j, i) for i, j in up]
        last = lax.slice_in_dim(x, length - width, length, axis=dim)
        initial = lax.slice_in_dim(x, 0, width, axis=dim)
        before = lax.ppermute(last, axis, up)
        after = lax.ppermute(initial, axis, down)
        x = jnp.concatenate([before, x, after], axis=dim)
    return x


def rows_first(field):
    return (
        field[..., :-4, :]
        - 8.0 * field[..., 1:-3, :]
        + 8.0 * field[..., 3:-1, :]
        - field[..., 4:, :]
    ) / 12.0


def cols_first(field):
    return (
        field[..., :-4] - 8.0 * field[..., 1:-3] + 8.0 * field[..., 3:-1] - field[..., 4:]
    ) / 12.0


def rows_second(field):
    return (
        -field[..., :-4, :]
        + 16.0 * field[..., 1:-3, :]
        - 30.0 * field[..., 2:-2, :]
        + 16.0 * field[..., 3:-1, :]
        - field[..., 4:, :]
    ) / 12.0


def second_column_split(field):
    return (
        -field[..., :-4]
        + 16.0 * field[..., 1:-3]
        - 30.0 * field[..., 2:-2]
        + 16.0 * field[..., 3:-1]
        - field[..., 4:]
    ) / 12.0


def surface(grad_a, grad_b, curve_aa, curve_bb, curve_ab):
    tan_a = (1.0 + grad_a[0], grad_a[1], grad_a[2])
    tan_b = (grad_b[0], 1.0 + grad_b[1], grad_b[2])
    normal = (
        tan_a[1] * tan_b[2] - tan_a[2] * tan_b[1],
        tan_a[2] * tan_b[0] - tan_a[0] * tan_b[2],
        tan_a[0] * tan_b[1] - tan_a[1] * tan_b[0],
    )
    area_stretch_factor = jnp.sqrt(
        normal[0] * normal[0] + normal[1] * normal[1] + normal[2] * normal[2]
    )
    unit = (
        normal[0] / area_stretch_factor,
        normal[1] / area_stretch_factor,
        normal[2] / area_stretch_factor,
    )
    first_edge_term = tan_a[0] * tan_a[0] + tan_a[1] * tan_a[1] + tan_a[2] * tan_a[2]
    first_f = tan_a[0] * tan_b[0] + tan_a[1] * tan_b[1] + tan_a[2] * tan_b[2]
    first_g = tan_b[0] * tan_b[0] + tan_b[1] * tan_b[1] + tan_b[2] * tan_b[2]
    second_l = curve_aa[0] * unit[0] + curve_aa[1] * unit[1] + curve_aa[2] * unit[2]
    second_m = curve_ab[0] * unit[0] + curve_ab[1] * unit[1] + curve_ab[2] * unit[2]
    second_n = curve_bb[0] * unit[0] + curve_bb[1] * unit[1] + curve_bb[2] * unit[2]
    curvature = (first_edge_term * second_n - 2.0 * first_f * second_m + first_g * second_l) / (
        2.0 * area_stretch_factor * area_stretch_factor
    )
    omega = (grad_a[3] / area_stretch_factor, grad_b[3] / area_stretch_factor)
    return (unit, curvature, omega)


def factors(length):
    inner = min(length, 256)
    return (length // inner, inner)


def angles(count_one, count_two, modulus):
    sample_lattice = (
        jnp.arange(count_one, dtype=jnp.int32)[:, None]
        * jnp.arange(count_two, dtype=jnp.int32)[None, :]
        % modulus
    )
    theta = sample_lattice.astype(jnp.float32) * (2.0 * math.pi / modulus)
    return (jnp.cos(theta), jnp.sin(theta))


def rotation(cos_table, sin_table, sense):
    top = jnp.stack([cos_table, sense * sin_table])
    low = jnp.stack([-sense * sin_table, cos_table])
    return jnp.stack([top, low])


def twisted(sheet_portion, cos_table, sin_table, sense):
    twist_re = sheet_portion[0] * cos_table + sense * sheet_portion[1] * sin_table
    twist_im = sheet_portion[1] * cos_table - sense * sheet_portion[0] * sin_table
    return jnp.stack([twist_re, twist_im])


def forward(values, length, kept, real_input):
    outer, inner = factors(length)
    cos_outer, sin_outer = angles(outer, outer, outer)
    if real_input:
        leading = values.shape[:-1]
        sample_lattice = values.reshape(leading + (outer, inner))
        lookup_array = jnp.stack([cos_outer, -sin_outer])
        sheet_portion = jnp.einsum(
            "...lm,zln->z...nm", sample_lattice, lookup_array, precision=largest_wavenumber
        )
    else:
        leading = values.shape[1:-1]
        sample_lattice = values.reshape((2,) + leading + (outer, inner))
        sheet_portion = jnp.einsum(
            "s...ab,tsac->t...cb",
            sample_lattice,
            rotation(cos_outer, sin_outer, 1.0),
            precision=largest_wavenumber,
        )
    cos_twist, sin_twist = angles(outer, inner, length)
    sheet_portion = twisted(sheet_portion, cos_twist, sin_twist, 1.0)
    cos_inner, sin_inner = angles(inner, kept, inner)
    result = jnp.einsum(
        "s...cb,tsbd->t...cd",
        sheet_portion,
        rotation(cos_inner, sin_inner, 1.0),
        precision=largest_wavenumber,
    )
    return result.reshape((2,) + leading + (outer * kept,))


def inverse(values, length, kept, want_imag):
    outer, inner = factors(length)
    leading = values.shape[1:-1]
    sample_lattice = values.reshape((2,) + leading + (outer, kept))
    cos_inner, sin_inner = angles(kept, inner, inner)
    sheet_portion = jnp.einsum(
        "s...cd,tsdb->t...cb",
        sample_lattice,
        rotation(cos_inner, sin_inner, -1.0),
        precision=largest_wavenumber,
    )
    cos_twist, sin_twist = angles(outer, inner, length)
    sheet_portion = twisted(sheet_portion, cos_twist, sin_twist, -1.0)
    cos_outer, sin_outer = angles(outer, outer, outer)
    if want_imag:
        result = jnp.einsum(
            "s...cb,tsca->t...ab",
            sheet_portion,
            rotation(cos_outer, sin_outer, -1.0),
            precision=largest_wavenumber,
        )
        return result.reshape((2,) + leading + (length,)) / length
    lookup_array = jnp.stack([cos_outer, -sin_outer])
    result = jnp.einsum(
        "s...cb,sca->...ab", sheet_portion, lookup_array, precision=largest_wavenumber
    )
    return result.reshape(leading + (length,)) / length


def wavenumbers(length, kept, positions):
    outer, inner = factors(length)
    number = positions // kept + outer * (positions % kept)
    signed = jnp.where(number >= length // 2, number - length, number)
    return (signed.astype(jnp.float32) / length, number == length // 2)


def local(shift_plane, height, dipole):
    fields = jnp.concatenate([shift_plane, height[None], dipole[None]], 0)
    padded = padded_2(fields, (("tr", 1), ("tc", 2)), 2)
    grad_a = rows_first(padded)[..., 2:-2]
    grad_b = cols_first(padded)[..., 2:-2, :]
    curve_aa = rows_second(padded[:3])[..., 2:-2]
    curve_bb = second_column_split(padded[:3])[..., 2:-2, :]
    curve_ab = rows_first(cols_first(padded[:3]))
    unit, curvature, omega = surface(grad_a, grad_b, curve_aa, curve_bb, curve_ab)
    vorticity = jnp.stack([omega[0], omega[1]])
    sheet_rows = lax.all_to_all(vorticity, "tc", split_axis=1, concat_axis=2, tiled=True)
    col_count = sheet_rows.shape[-1]
    row_count = height.shape[0] * lax.axis_size("tr")
    col_outer, col_inner = factors(col_count)
    row_outer, row_inner = factors(row_count)
    kept = col_inner // 2
    row_spec = forward(sheet_rows, col_count, kept, True)
    stacked = row_spec.reshape((4,) + row_spec.shape[2:])
    columns = lax.all_to_all(stacked, ("tr", "tc"), split_axis=2, concat_axis=1, tiled=True)
    columns = jnp.swapaxes(columns, 1, 2)
    local_width = columns.shape[1]
    full = forward(columns.reshape((2, 2) + columns.shape[1:]), row_count, row_inner, False)
    complete_real_part = full[0]
    full_im = full[1]
    place = lax.axis_index(("tr", "tc")) * local_width + jnp.arange(local_width, dtype=jnp.int32)
    freq_two, nyquist_two = wavenumbers(col_count, kept, place)
    freq_one, nyquist_one = wavenumbers(
        row_count, row_inner, jnp.arange(row_count, dtype=jnp.int32)
    )
    freq_one = freq_one[None, :]
    freq_two = freq_two[:, None]
    radius = jnp.sqrt(freq_one * freq_one + freq_two * freq_two)
    live = (
        jnp.logical_not(nyquist_one[None, :])
        & jnp.logical_not(nyquist_two[:, None])
        & (radius > 0.0)
    )
    factor = jnp.where(live, 0.5 / jnp.where(live, radius, 1.0), 0.0)
    summed_re = factor * (freq_one * complete_real_part[0] + freq_two * complete_real_part[1])
    summed_im = factor * (freq_one * full_im[0] + freq_two * full_im[1])
    speed_parts = inverse(jnp.stack([summed_im, -summed_re]), row_count, row_inner, True)
    partial_value = jnp.swapaxes(speed_parts, 1, 2)
    back_rows = lax.all_to_all(partial_value, ("tr", "tc"), split_axis=1, concat_axis=2, tiled=True)
    weights = (
        jnp.full((col_outer, kept), 2.0, jnp.float32).at[0, 0].set(1.0).reshape(col_outer * kept)
    )
    speed_rows = inverse(back_rows * weights, col_count, kept, False)
    speed = lax.all_to_all(speed_rows, "tc", split_axis=1, concat_axis=0, tiled=True)
    velocity_update = jnp.stack([speed * unit[0], speed * unit[1], speed * unit[2]])
    dipole_update = -2.0 * 0.5 * 0.5 * height + 0.3 * curvature + 0.5 * speed * speed
    return (velocity_update, dipole_update)


LANES = 128
SUB = 8
VMEM_BYTES = 58 * 1024 * 1024


def params():
    return pltpu.CompilerParams(vmem_limit_bytes=VMEM_BYTES)


def two_halves(table):
    table = np.asarray(table, np.float32)
    high = table.astype(jnp.bfloat16)
    low = (table - high.astype(np.float32)).astype(jnp.bfloat16)
    return np.stack([high, low])


def unit_circle(count_one, count_two, modulus):
    theta = np.arange(count_one)[:, None] * np.arange(count_two)[None, :] % modulus
    theta = theta * (2.0 * math.pi / modulus)
    return np.cos(theta), np.sin(theta)


def split(x):
    high = x.astype(jnp.bfloat16)
    low = (x - high.astype(jnp.float32)).astype(jnp.bfloat16)
    return high, low


def product(a, b):
    dot = lambda p, q: jnp.dot(p, q, preferred_element_type=jnp.float32)
    return dot(a[0], b[0]) + (dot(a[0], b[1]) + dot(a[1], b[0]))


def plus(p, q):
    return q if p is None else p if q is None else p + q


def minus(p, q):
    if q is None:
        return p
    return -q if p is None else p - q


def turned(z, number, size, sense):
    re, im = z
    number = number % size
    if number == 0:
        return z
    if 4 * number == size:
        if sense > 0:
            return (im, None if re is None else -re)
        return (None if im is None else -im, re)
    c = math.cos(2.0 * math.pi * number / size)
    s = -sense * math.sin(2.0 * math.pi * number / size)
    if 8 * number == size:
        r = math.sqrt(0.5)
        if im is None:
            return (re * r, re * (-sense * r))
        if sense > 0:
            return ((re + im) * r, (im - re) * r)
        return ((re - im) * r, (im + re) * r)
    if im is None:
        return (re * c, re * s)
    return (re * c - im * s, re * s + im * c)


def butterflies(z, sense):
    size = len(z)
    if size == 1:
        return z
    even = butterflies(z[0::2], sense)
    odd = butterflies(z[1::2], sense)
    odd = [turned(o, k, size, sense) for k, o in enumerate(odd)]
    head = [(plus(e[0], o[0]), plus(e[1], o[1])) for e, o in zip(even, odd)]
    tail = [(minus(e[0], o[0]), minus(e[1], o[1])) for e, o in zip(even, odd)]
    return head + tail


def twist(z, c, s, sense):
    re, im = z
    if im is None:
        return (re * c, re * s * (-sense))
    if sense > 0:
        return (re * c + im * s, im * c - re * s)
    return (re * c - im * s, im * c + re * s)


def stencil(shift_plane, height, dipole, halos, tc, want_omega):
    rows, cols = height.shape
    block = min(64, rows // tc)
    steps = rows // block
    chunk = min(256, cols)
    wide = min(1024, cols)
    groups = block // SUB
    count = 4 if want_omega else 3
    tall = block + 2 * SUB
    last = rows // SUB - 1

    def kernel(*refs):
        if want_omega:
            arrays, refs = (refs[:9], refs[9:])
            top, bottom, left, right, omega_ref, pad, slope = refs
        else:
            arrays, refs = (refs[:6], refs[6:])
            top, bottom, left, right, unit_ref, base_ref, pad, slope, bend = refs
        i = pl.program_id(0)
        for f in range(count):
            trio = arrays[:3] if f < 2 else arrays[3 * (f - 1) : 3 * f]
            take = (lambda r: r[f]) if f < 2 else (lambda r: r[...])
            cur, prev, nxt = trio
            pad[f, SUB : SUB + block, LANES : LANES + cols] = take(cur)
            pad[f, 0:SUB, LANES : LANES + cols] = jnp.where(i == 0, top[f], take(prev))
            pad[f, SUB + block :, LANES : LANES + cols] = jnp.where(
                i == steps - 1, bottom[f], take(nxt)
            )
            pad[f, :, 0:LANES] = left[f, pl.ds(pl.multiple_of(i * block, SUB), tall), :]
            pad[f, :, LANES + cols :] = right[f, pl.ds(pl.multiple_of(i * block, SUB), tall), :]

        def along(g, carry):
            r = pl.ds(pl.multiple_of(g * SUB, SUB), SUB)
            for f in range(count):
                for j in range(cols // wide):
                    width = wide + 2 * LANES
                    x = pad[f, r, j * wide : j * wide + width]
                    roll = lambda k: pltpu.roll(x, k % width, 1)[:, LANES : LANES + wide]
                    m2, m1, p1, p2 = roll(2), roll(1), roll(-1), roll(-2)
                    here = slice(j * wide, (j + 1) * wide)
                    slope[f, r, here] = ((m2 - p2) + 8.0 * (p1 - m1)) * (1.0 / 12.0)
                    if not want_omega:
                        mid = x[:, LANES : LANES + wide]
                        bend[f, r, here] = (16.0 * (m1 + p1) - (m2 + p2) - 30.0 * mid) * (
                            1.0 / 12.0
                        )
            return carry

        lax.fori_loop(0, tall // SUB, along, 0)

        def across(j, carry):
            inner = pl.ds(pl.multiple_of(j * chunk, LANES), chunk)
            outer = pl.ds(pl.multiple_of(j * chunk + LANES, LANES), chunk)
            for g in range(groups):
                at = lambda ref, f, k, lanes: ref[f, SUB * (g + 1) + k : SUB * (g + 2) + k, lanes]

                def first(ref, f, lanes):
                    return (
                        (at(ref, f, -2, lanes) - at(ref, f, 2, lanes))
                        + 8.0 * (at(ref, f, 1, lanes) - at(ref, f, -1, lanes))
                    ) * (1.0 / 12.0)

                ga = [first(pad, f, outer) for f in range(count)]
                gb = [at(slope, f, 0, inner) for f in range(count)]
                ta = (1.0 + ga[0], ga[1], ga[2])
                tb = (gb[0], 1.0 + gb[1], gb[2])
                n = (
                    ta[1] * tb[2] - ta[2] * tb[1],
                    ta[2] * tb[0] - ta[0] * tb[2],
                    ta[0] * tb[1] - ta[1] * tb[0],
                )
                inv = 1.0 / jnp.sqrt(n[0] * n[0] + n[1] * n[1] + n[2] * n[2])
                out = slice(g * SUB, (g + 1) * SUB)
                if want_omega:
                    omega_ref[0, 0, out, inner] = ga[3] * inv
                    omega_ref[0, 1, out, inner] = gb[3] * inv
                    continue
                unit = [v * inv for v in n]
                for f in range(3):
                    unit_ref[f, out, inner] = unit[f]
                big_e = ta[0] * ta[0] + ta[1] * ta[1] + ta[2] * ta[2]
                big_f = ta[0] * tb[0] + ta[1] * tb[1] + ta[2] * tb[2]
                big_g = tb[0] * tb[0] + tb[1] * tb[1] + tb[2] * tb[2]
                sl = sm = sn = None
                for f in range(3):
                    mid = at(pad, f, 0, outer)
                    aa = (
                        16.0 * (at(pad, f, -1, outer) + at(pad, f, 1, outer))
                        - (at(pad, f, -2, outer) + at(pad, f, 2, outer))
                        - 30.0 * mid
                    ) * (1.0 / 12.0)
                    sl = plus(sl, aa * unit[f])
                    sm = plus(sm, first(slope, f, inner) * unit[f])
                    sn = plus(sn, at(bend, f, 0, inner) * unit[f])
                curvature = (big_e * sn - 2.0 * big_f * sm + big_g * sl) * (0.5 * inv * inv)
                base_ref[out, inner] = -0.5 * at(pad, 2, 0, outer) + 0.3 * curvature
            return carry

        lax.fori_loop(0, cols // chunk, across, 0)

    per = block // SUB
    plane = [
        pl.BlockSpec((block, cols), lambda i: (i, 0)),
        pl.BlockSpec((SUB, cols), lambda i: (jnp.maximum(i * per - 1, 0), 0)),
        pl.BlockSpec((SUB, cols), lambda i: (jnp.minimum((i + 1) * per, last), 0)),
    ]
    pair = [
        pl.BlockSpec((2, block, cols), lambda i: (0, i, 0)),
        pl.BlockSpec((2, SUB, cols), lambda i: (0, jnp.maximum(i * per - 1, 0), 0)),
        pl.BlockSpec((2, SUB, cols), lambda i: (0, jnp.minimum((i + 1) * per, last), 0)),
    ]
    whole = [pl.BlockSpec(h.shape, lambda i: (0, 0, 0)) for h in halos]
    ins = [shift_plane] * 3 + [height] * 3 + ([dipole] * 3 if want_omega else [])
    scratch = [
        pltpu.VMEM((count, tall, cols + 2 * LANES), jnp.float32),
        pltpu.VMEM((count, tall, cols), jnp.float32),
    ]
    f32 = lambda *dims: jax.ShapeDtypeStruct(dims, jnp.float32)
    if want_omega:
        half = steps // tc
        out_shape = f32(tc, 2, rows // tc, cols)
        out_specs = pl.BlockSpec((1, 2, block, cols), lambda i: (i // half, 0, i % half, 0))
    else:
        out_shape = (f32(3, rows, cols), f32(rows, cols))
        out_specs = (
            pl.BlockSpec((3, block, cols), lambda i: (0, i, 0)),
            pl.BlockSpec((block, cols), lambda i: (i, 0)),
        )
        scratch.append(pltpu.VMEM((count, tall, cols), jnp.float32))
    return pl.pallas_call(
        kernel,
        grid=(steps,),
        in_specs=pair + plane * (count - 2) + whole,
        out_specs=out_specs,
        out_shape=out_shape,
        scratch_shapes=scratch,
        compiler_params=params(),
        name="omega" if want_omega else "geometry",
    )(*ins, *halos)


def row_tables(outer, inner, length):
    c, s = unit_circle(outer, inner, length)
    table = np.stack([c, s]).astype(np.float32)
    return jnp.broadcast_to(jnp.asarray(table)[:, :, None, :], (2, outer, SUB, inner))


def row_forward(omega, outer, inner):
    tc, _, rows, cols = omega.shape
    kept = inner // 2
    length = tc * cols
    block = min(64, rows)
    per = outer // tc
    c, s = unit_circle(inner, kept, inner)
    matrix = two_halves(np.block([[c, -s], [s, c]]))

    def kernel(x_ref, tw_ref, m_ref, out_ref, mid):
        def step(g, carry):
            r = pl.ds(pl.multiple_of(g * SUB, SUB), SUB)
            for j in range(0, inner, LANES):
                z = []
                for l in range(outer):
                    at = (l % per) * inner + j
                    z.append((x_ref[l // per, 0, r, at : at + LANES], None))
                z = butterflies(z, 1.0)
                for n in range(outer):
                    re, im = z[n]
                    if n:
                        re, im = twist(
                            z[n],
                            tw_ref[0, n, :, j : j + LANES],
                            tw_ref[1, n, :, j : j + LANES],
                            1.0,
                        )
                    if im is None:
                        im = jnp.zeros_like(re)
                    mid[n, r, j : j + LANES] = re
                    mid[n, r, inner + j : inner + j + LANES] = im
            return carry

        lax.fori_loop(0, block // SUB, step, 0)

        def finish(n, carry):
            y = product(split(mid[n]), (m_ref[0], m_ref[1]))
            out_ref[n, 0, 0] = y[:, :kept]
            out_ref[n, 1, 0] = y[:, kept:]
            return carry

        lax.fori_loop(0, outer, finish, 0, unroll=4)

    return pl.pallas_call(
        kernel,
        grid=(2, rows // block),
        in_specs=[
            pl.BlockSpec((tc, 1, block, cols), lambda p, i: (0, p, i, 0)),
            pl.BlockSpec((2, outer, SUB, inner), lambda p, i: (0, 0, 0, 0)),
            pl.BlockSpec(matrix.shape, lambda p, i: (0, 0, 0)),
        ],
        out_specs=pl.BlockSpec((outer, 2, 1, block, kept), lambda p, i: (0, 0, p, i, 0)),
        out_shape=jax.ShapeDtypeStruct((outer, 2, 2, rows, kept), jnp.float32),
        scratch_shapes=[pltpu.VMEM((outer, block, 2 * inner), jnp.float32)],
        compiler_params=params(),
        name="rows_forward",
    )(omega, row_tables(outer, inner, length), jnp.asarray(matrix))


def column_middle(spectra, freq_two, live_two, outer, inner):
    length = outer * inner
    width = spectra.shape[-1]
    c, s = unit_circle(outer, inner, length)
    table = jnp.asarray(np.stack([c, s]).astype(np.float32))
    table = jnp.broadcast_to(table[..., None], (2, outer, inner, width))
    c, s = unit_circle(inner, inner, inner)
    matrix = two_halves(np.concatenate([c, s], 0))

    def kernel(x_ref, tw_ref, m_ref, f_ref, live_ref, out_ref, mid):
        def down(g, carry):
            r = pl.ds(pl.multiple_of(g * SUB, SUB), SUB)
            for p in range(2):
                z = [(x_ref[a, 0, p, r, :], x_ref[a, 1, p, r, :]) for a in range(outer)]
                z = butterflies(z, 1.0)
                for k in range(outer):
                    re, im = z[k] if k == 0 else twist(z[k], tw_ref[0, k, r], tw_ref[1, k, r], 1.0)
                    mid[k, r, (2 * p) * width : (2 * p + 1) * width] = re
                    mid[k, r, (2 * p + 1) * width : (2 * p + 2) * width] = im
            return carry

        lax.fori_loop(0, inner // SUB, down, 0)
        fre_two = f_ref[...]
        live_cols = live_ref[...]
        weights = (m_ref[0], m_ref[1])

        def turn(k, carry):
            y = product(weights, split(mid[k]))
            parts = []
            for p in range(2):
                lo = slice((2 * p) * width, (2 * p + 1) * width)
                hi = slice((2 * p + 1) * width, (2 * p + 2) * width)
                parts.append((y[:inner, lo] + y[inner:, hi], y[:inner, hi] - y[inner:, lo]))
            number = k + outer * lax.broadcasted_iota(jnp.int32, (inner, width), 0)
            signed = jnp.where(number >= length // 2, number - length, number)
            fre_one = signed.astype(jnp.float32) * (1.0 / length)
            radius = jnp.sqrt(fre_one * fre_one + fre_two * fre_two)
            live = (number != length // 2) & (live_cols > 0.0) & (radius > 0.0)
            factor = jnp.where(live, 0.5 / jnp.where(live, radius, 1.0), 0.0)
            one = factor * fre_one
            two = factor * fre_two
            sum_re = one * parts[0][0] + two * parts[1][0]
            sum_im = one * parts[0][1] + two * parts[1][1]
            w = jnp.concatenate([sum_im, -sum_re], 1)
            y = product(weights, split(w))
            mid[k, :, :width] = y[:inner, :width] - y[inner:, width:]
            mid[k, :, width : 2 * width] = y[:inner, width:] + y[inner:, :width]
            return carry

        lax.fori_loop(0, outer, turn, 0)

        def up(g, carry):
            r = pl.ds(pl.multiple_of(g * SUB, SUB), SUB)
            z = []
            for k in range(outer):
                v = (mid[k, r, :width], mid[k, r, width : 2 * width])
                z.append(v if k == 0 else twist(v, tw_ref[0, k, r], tw_ref[1, k, r], -1.0))
            z = butterflies(z, -1.0)
            for a in range(outer):
                out_ref[a, 0, r, :] = z[a][0] * (1.0 / length)
                out_ref[a, 1, r, :] = z[a][1] * (1.0 / length)
            return carry

        lax.fori_loop(0, inner // SUB, up, 0)

    return pl.pallas_call(
        kernel,
        out_shape=jax.ShapeDtypeStruct((outer, 2, inner, width), jnp.float32),
        scratch_shapes=[pltpu.VMEM((outer, inner, 4 * width), jnp.float32)],
        compiler_params=params(),
        name="columns",
    )(spectra, table, jnp.asarray(matrix), freq_two, live_two)


def row_inverse(partial, outer, inner, tc):
    _, _, rows, kept = partial.shape
    length = outer * inner
    cols = length // tc
    per = outer // tc
    block = min(64, rows)
    c, s = unit_circle(kept, inner, inner)
    matrix = two_halves(np.block([[c, s], [-s, c]]) * (2.0 / length))

    def kernel(x_ref, tw_ref, m_ref, out_ref, mid):
        lane = lax.broadcasted_iota(jnp.int32, (block, kept), 1)

        def start(n, carry):
            weight = jnp.where((lane == 0) & (n == 0), 0.5, 1.0)
            w = jnp.concatenate([x_ref[n, 0] * weight, x_ref[n, 1] * weight], 1)
            mid[n] = product(split(w), (m_ref[0], m_ref[1]))
            return carry

        lax.fori_loop(0, outer, start, 0, unroll=4)

        def step(g, carry):
            r = pl.ds(pl.multiple_of(g * SUB, SUB), SUB)
            for j in range(0, inner, LANES):
                z = []
                for n in range(outer):
                    v = (mid[n, r, j : j + LANES], mid[n, r, inner + j : inner + j + LANES])
                    if n:
                        v = twist(
                            v,
                            tw_ref[0, n, :, j : j + LANES],
                            tw_ref[1, n, :, j : j + LANES],
                            -1.0,
                        )
                    z.append(v)
                z = butterflies(z, -1.0)
                for l in range(outer):
                    at = (l % per) * inner + j
                    out_ref[l // per, r, at : at + LANES] = z[l][0]
            return carry

        lax.fori_loop(0, block // SUB, step, 0)

    return pl.pallas_call(
        kernel,
        grid=(rows // block,),
        in_specs=[
            pl.BlockSpec((outer, 2, block, kept), lambda i: (0, 0, i, 0)),
            pl.BlockSpec((2, outer, SUB, inner), lambda i: (0, 0, 0, 0)),
            pl.BlockSpec(matrix.shape, lambda i: (0, 0, 0)),
        ],
        out_specs=pl.BlockSpec((tc, block, cols), lambda i: (0, i, 0)),
        out_shape=jax.ShapeDtypeStruct((tc, rows, cols), jnp.float32),
        scratch_shapes=[pltpu.VMEM((outer, block, 2 * inner), jnp.float32)],
        compiler_params=params(),
        name="rows_inverse",
    )(partial, row_tables(outer, inner, length), jnp.asarray(matrix))


def ring(axis):
    devices = lax.axis_size(axis)
    up = [(i, (i + 1) % devices) for i in range(devices)]
    return up, [(j, i) for i, j in up]


def edges(shift_plane, height, dipole):
    fields = lambda cut: jnp.concatenate([cut(shift_plane), cut(height[None]), cut(dipole[None])], 0)
    up, down = ring("tr")
    top = lax.ppermute(fields(lambda x: x[:, -SUB:]), "tr", up)
    bottom = lax.ppermute(fields(lambda x: x[:, :SUB]), "tr", down)

    def slab(lanes):
        body = fields(lambda x: x[..., lanes])
        return jnp.concatenate([top[..., lanes], body, bottom[..., lanes]], 1)

    up, down = ring("tc")
    left = lax.ppermute(slab(slice(-LANES, None)), "tc", up)
    right = lax.ppermute(slab(slice(0, LANES)), "tc", down)
    return top, bottom, left, right


def local_kernels(shift_plane, height, dipole):
    tc = lax.axis_size("tc")
    rows, cols = height.shape
    col_outer, col_inner = factors(cols * tc)
    row_outer, row_inner = factors(rows * lax.axis_size("tr"))
    kept = col_inner // 2
    halos = edges(shift_plane, height, dipole)
    omega = stencil(shift_plane, height, dipole, halos, tc, True)
    omega = lax.all_to_all(omega, "tc", split_axis=0, concat_axis=0, tiled=True)
    spectra = row_forward(omega, col_outer, col_inner)
    spectra = lax.all_to_all(spectra, ("tr", "tc"), split_axis=0, concat_axis=0, tiled=True)
    unit, base = stencil(shift_plane, height, dipole, halos, tc, False)
    place = lax.axis_index(("tr", "tc")) * kept + jnp.arange(kept, dtype=jnp.int32)
    freq_two, nyquist_two = wavenumbers(cols * tc, kept, place)
    live_two = jnp.where(nyquist_two, 0.0, 1.0)
    partial = column_middle(spectra, freq_two[None, :], live_two[None, :], row_outer, row_inner)
    partial = lax.all_to_all(partial, ("tr", "tc"), split_axis=0, concat_axis=0, tiled=True)
    speed = row_inverse(partial, col_outer, col_inner, tc)
    speed = lax.all_to_all(speed, "tc", split_axis=0, concat_axis=0, tiled=True)
    speed = speed.reshape(rows, cols)
    return (speed[None] * unit, base + 0.5 * speed * speed)


def fits(rows, cols, tr, tc):
    col_outer, col_inner = factors(cols * tc)
    row_outer, row_inner = factors(rows * tr)
    peers = tr * tc
    return (
        tc > 1
        and col_outer == row_outer == peers == 16
        and col_inner // 2 == LANES
        and rows // tc == row_inner
        and rows % (SUB * tc) == 0
        and col_outer % tc == 0
    )


def solution(mesh):
    in_specs = (
        P(None, ("groups", "tr"), "tc"),
        P(("groups", "tr"), "tc"),
        P(("groups", "tr"), "tc"),
    )
    out_specs = (P(None, ("groups", "tr"), "tc"), P(("groups", "tr"), "tc"))

    def chosen(shift_plane, height, dipole):
        rows, cols = height.shape
        if fits(rows, cols, lax.axis_size("tr"), lax.axis_size("tc")):
            return local_kernels(shift_plane, height, dipole)
        return local(shift_plane, height, dipole)

    return jax.shard_map(chosen, mesh=mesh, in_specs=in_specs, out_specs=out_specs, check_vma=False)
```

```python
import math

import jax
import jax.numpy as jnp
import numpy as np
from jax import lax
from jax.experimental import pallas as pl
from jax.experimental.pallas import tpu as pltpu
from jax.sharding import PartitionSpec as P

largest_wavenumber = lax.Precision.HIGHEST


def padded_2(x, sides, width):
    for axis, dim in sides:
        devices, length = (lax.axis_size(axis), x.shape[dim])
        up = [(i, (i + 1) % devices) for i in range(devices)]
        down = [(j, i) for i, j in up]
        last = lax.slice_in_dim(x, length - width, length, axis=dim)
        initial = lax.slice_in_dim(x, 0, width, axis=dim)
        before = lax.ppermute(last, axis, up)
        after = lax.ppermute(initial, axis, down)
        x = jnp.concatenate([before, x, after], axis=dim)
    return x


def rows_first(field):
    return (
        field[..., :-4, :]
        - 8.0 * field[..., 1:-3, :]
        + 8.0 * field[..., 3:-1, :]
        - field[..., 4:, :]
    ) / 12.0


def cols_first(field):
    return (
        field[..., :-4] - 8.0 * field[..., 1:-3] + 8.0 * field[..., 3:-1] - field[..., 4:]
    ) / 12.0


def rows_second(field):
    return (
        -field[..., :-4, :]
        + 16.0 * field[..., 1:-3, :]
        - 30.0 * field[..., 2:-2, :]
        + 16.0 * field[..., 3:-1, :]
        - field[..., 4:, :]
    ) / 12.0


def second_column_split(field):
    return (
        -field[..., :-4]
        + 16.0 * field[..., 1:-3]
        - 30.0 * field[..., 2:-2]
        + 16.0 * field[..., 3:-1]
        - field[..., 4:]
    ) / 12.0


def surface(grad_a, grad_b, curve_aa, curve_bb, curve_ab):
    tan_a = (1.0 + grad_a[0], grad_a[1], grad_a[2])
    tan_b = (grad_b[0], 1.0 + grad_b[1], grad_b[2])
    normal = (
        tan_a[1] * tan_b[2] - tan_a[2] * tan_b[1],
        tan_a[2] * tan_b[0] - tan_a[0] * tan_b[2],
        tan_a[0] * tan_b[1] - tan_a[1] * tan_b[0],
    )
    area_stretch_factor = jnp.sqrt(
        normal[0] * normal[0] + normal[1] * normal[1] + normal[2] * normal[2]
    )
    unit = (
        normal[0] / area_stretch_factor,
        normal[1] / area_stretch_factor,
        normal[2] / area_stretch_factor,
    )
    first_edge_term = tan_a[0] * tan_a[0] + tan_a[1] * tan_a[1] + tan_a[2] * tan_a[2]
    first_f = tan_a[0] * tan_b[0] + tan_a[1] * tan_b[1] + tan_a[2] * tan_b[2]
    first_g = tan_b[0] * tan_b[0] + tan_b[1] * tan_b[1] + tan_b[2] * tan_b[2]
    second_l = curve_aa[0] * unit[0] + curve_aa[1] * unit[1] + curve_aa[2] * unit[2]
    second_m = curve_ab[0] * unit[0] + curve_ab[1] * unit[1] + curve_ab[2] * unit[2]
    second_n = curve_bb[0] * unit[0] + curve_bb[1] * unit[1] + curve_bb[2] * unit[2]
    curvature = (first_edge_term * second_n - 2.0 * first_f * second_m + first_g * second_l) / (
        2.0 * area_stretch_factor * area_stretch_factor
    )
    omega = (grad_a[3] / area_stretch_factor, grad_b[3] / area_stretch_factor)
    return (unit, curvature, omega)


def factors(length):
    inner = min(length, 256)
    return (length // inner, inner)


def angles(count_one, count_two, modulus):
    sample_lattice = (
        jnp.arange(count_one, dtype=jnp.int32)[:, None]
        * jnp.arange(count_two, dtype=jnp.int32)[None, :]
        % modulus
    )
    theta = sample_lattice.astype(jnp.float32) * (2.0 * math.pi / modulus)
    return (jnp.cos(theta), jnp.sin(theta))


def rotation(cos_table, sin_table, sense):
    top = jnp.stack([cos_table, sense * sin_table])
    low = jnp.stack([-sense * sin_table, cos_table])
    return jnp.stack([top, low])


def twisted(sheet_portion, cos_table, sin_table, sense):
    twist_re = sheet_portion[0] * cos_table + sense * sheet_portion[1] * sin_table
    twist_im = sheet_portion[1] * cos_table - sense * sheet_portion[0] * sin_table
    return jnp.stack([twist_re, twist_im])


def forward(values, length, kept, real_input):
    outer, inner = factors(length)
    cos_outer, sin_outer = angles(outer, outer, outer)
    if real_input:
        leading = values.shape[:-1]
        sample_lattice = values.reshape(leading + (outer, inner))
        lookup_array = jnp.stack([cos_outer, -sin_outer])
        sheet_portion = jnp.einsum(
            "...lm,zln->z...nm", sample_lattice, lookup_array, precision=largest_wavenumber
        )
    else:
        leading = values.shape[1:-1]
        sample_lattice = values.reshape((2,) + leading + (outer, inner))
        sheet_portion = jnp.einsum(
            "s...ab,tsac->t...cb",
            sample_lattice,
            rotation(cos_outer, sin_outer, 1.0),
            precision=largest_wavenumber,
        )
    cos_twist, sin_twist = angles(outer, inner, length)
    sheet_portion = twisted(sheet_portion, cos_twist, sin_twist, 1.0)
    cos_inner, sin_inner = angles(inner, kept, inner)
    result = jnp.einsum(
        "s...cb,tsbd->t...cd",
        sheet_portion,
        rotation(cos_inner, sin_inner, 1.0),
        precision=largest_wavenumber,
    )
    return result.reshape((2,) + leading + (outer * kept,))


def inverse(values, length, kept, want_imag):
    outer, inner = factors(length)
    leading = values.shape[1:-1]
    sample_lattice = values.reshape((2,) + leading + (outer, kept))
    cos_inner, sin_inner = angles(kept, inner, inner)
    sheet_portion = jnp.einsum(
        "s...cd,tsdb->t...cb",
        sample_lattice,
        rotation(cos_inner, sin_inner, -1.0),
        precision=largest_wavenumber,
    )
    cos_twist, sin_twist = angles(outer, inner, length)
    sheet_portion = twisted(sheet_portion, cos_twist, sin_twist, -1.0)
    cos_outer, sin_outer = angles(outer, outer, outer)
    if want_imag:
        result = jnp.einsum(
            "s...cb,tsca->t...ab",
            sheet_portion,
            rotation(cos_outer, sin_outer, -1.0),
            precision=largest_wavenumber,
        )
        return result.reshape((2,) + leading + (length,)) / length
    lookup_array = jnp.stack([cos_outer, -sin_outer])
    result = jnp.einsum(
        "s...cb,sca->...ab", sheet_portion, lookup_array, precision=largest_wavenumber
    )
    return result.reshape(leading + (length,)) / length


def wavenumbers(length, kept, positions):
    outer, inner = factors(length)
    number = positions // kept + outer * (positions % kept)
    signed = jnp.where(number >= length // 2, number - length, number)
    return (signed.astype(jnp.float32) / length, number == length // 2)


def local(shift_plane, height, dipole):
    fields = jnp.concatenate([shift_plane, height[None], dipole[None]], 0)
    padded = padded_2(fields, (("tr", 1), ("tc", 2)), 2)
    grad_a = rows_first(padded)[..., 2:-2]
    grad_b = cols_first(padded)[..., 2:-2, :]
    curve_aa = rows_second(padded[:3])[..., 2:-2]
    curve_bb = second_column_split(padded[:3])[..., 2:-2, :]
    curve_ab = rows_first(cols_first(padded[:3]))
    unit, curvature, omega = surface(grad_a, grad_b, curve_aa, curve_bb, curve_ab)
    vorticity = jnp.stack([omega[0], omega[1]])
    sheet_rows = lax.all_to_all(vorticity, "tc", split_axis=1, concat_axis=2, tiled=True)
    col_count = sheet_rows.shape[-1]
    row_count = height.shape[0] * lax.axis_size("tr")
    col_outer, col_inner = factors(col_count)
    row_outer, row_inner = factors(row_count)
    kept = col_inner // 2
    row_spec = forward(sheet_rows, col_count, kept, True)
    stacked = row_spec.reshape((4,) + row_spec.shape[2:])
    columns = lax.all_to_all(stacked, ("tr", "tc"), split_axis=2, concat_axis=1, tiled=True)
    columns = jnp.swapaxes(columns, 1, 2)
    local_width = columns.shape[1]
    full = forward(columns.reshape((2, 2) + columns.shape[1:]), row_count, row_inner, False)
    complete_real_part = full[0]
    full_im = full[1]
    place = lax.axis_index(("tr", "tc")) * local_width + jnp.arange(local_width, dtype=jnp.int32)
    freq_two, nyquist_two = wavenumbers(col_count, kept, place)
    freq_one, nyquist_one = wavenumbers(
        row_count, row_inner, jnp.arange(row_count, dtype=jnp.int32)
    )
    freq_one = freq_one[None, :]
    freq_two = freq_two[:, None]
    radius = jnp.sqrt(freq_one * freq_one + freq_two * freq_two)
    live = (
        jnp.logical_not(nyquist_one[None, :])
        & jnp.logical_not(nyquist_two[:, None])
        & (radius > 0.0)
    )
    factor = jnp.where(live, 0.5 / jnp.where(live, radius, 1.0), 0.0)
    summed_re = factor * (freq_one * complete_real_part[0] + freq_two * complete_real_part[1])
    summed_im = factor * (freq_one * full_im[0] + freq_two * full_im[1])
    speed_parts = inverse(jnp.stack([summed_im, -summed_re]), row_count, row_inner, True)
    partial_value = jnp.swapaxes(speed_parts, 1, 2)
    back_rows = lax.all_to_all(partial_value, ("tr", "tc"), split_axis=1, concat_axis=2, tiled=True)
    weights = (
        jnp.full((col_outer, kept), 2.0, jnp.float32).at[0, 0].set(1.0).reshape(col_outer * kept)
    )
    speed_rows = inverse(back_rows * weights, col_count, kept, False)
    speed = lax.all_to_all(speed_rows, "tc", split_axis=1, concat_axis=0, tiled=True)
    velocity_update = jnp.stack([speed * unit[0], speed * unit[1], speed * unit[2]])
    dipole_update = -2.0 * 0.5 * 0.5 * height + 0.3 * curvature + 0.5 * speed * speed
    return (velocity_update, dipole_update)


LANES = 128
SUB = 8
VMEM_BYTES = 58 * 1024 * 1024


def params():
    return pltpu.CompilerParams(vmem_limit_bytes=VMEM_BYTES)


def two_halves(table):
    table = np.asarray(table, np.float32)
    high = table.astype(jnp.bfloat16)
    low = (table - high.astype(np.float32)).astype(jnp.bfloat16)
    return np.stack([high, low])


def unit_circle(count_one, count_two, modulus):
    theta = np.arange(count_one)[:, None] * np.arange(count_two)[None, :] % modulus
    theta = theta * (2.0 * math.pi / modulus)
    return np.cos(theta), np.sin(theta)


def split(x):
    high = x.astype(jnp.bfloat16)
    low = (x - high.astype(jnp.float32)).astype(jnp.bfloat16)
    return high, low


def product(a, b):
    dot = lambda p, q: jnp.dot(p, q, preferred_element_type=jnp.float32)
    return dot(a[0], b[0]) + (dot(a[0], b[1]) + dot(a[1], b[0]))


def plus(p, q):
    return q if p is None else p if q is None else p + q


def minus(p, q):
    if q is None:
        return p
    return -q if p is None else p - q


def turned(z, number, size, sense):
    re, im = z
    number = number % size
    if number == 0:
        return z
    if 4 * number == size:
        if sense > 0:
            return (im, None if re is None else -re)
        return (None if im is None else -im, re)
    c = math.cos(2.0 * math.pi * number / size)
    s = -sense * math.sin(2.0 * math.pi * number / size)
    if 8 * number == size:
        r = math.sqrt(0.5)
        if im is None:
            return (re * r, re * (-sense * r))
        if sense > 0:
            return ((re + im) * r, (im - re) * r)
        return ((re - im) * r, (im + re) * r)
    if im is None:
        return (re * c, re * s)
    return (re * c - im * s, re * s + im * c)


def butterflies(z, sense):
    size = len(z)
    if size == 1:
        return z
    even = butterflies(z[0::2], sense)
    odd = butterflies(z[1::2], sense)
    odd = [turned(o, k, size, sense) for k, o in enumerate(odd)]
    head = [(plus(e[0], o[0]), plus(e[1], o[1])) for e, o in zip(even, odd)]
    tail = [(minus(e[0], o[0]), minus(e[1], o[1])) for e, o in zip(even, odd)]
    return head + tail


def twist(z, c, s, sense):
    re, im = z
    if im is None:
        return (re * c, re * s * (-sense))
    if sense > 0:
        return (re * c + im * s, im * c - re * s)
    return (re * c - im * s, im * c + re * s)


def stencil(shift_plane, height, dipole, halos, tc, want_omega, part, parts, earlier=()):
    rows, cols = height.shape
    block = min(64, rows // (tc * parts))
    steps = rows // (block * parts)
    ahead = part * steps
    chunk = min(128, cols)
    wide = min(1024, cols)
    groups = block // SUB
    count = 4 if want_omega else 3
    tall = block + 2 * SUB
    last = rows // SUB - 1

    def kernel(*refs):
        if want_omega:
            arrays, refs = (refs[:9], refs[9:])
            top, bottom, left, right, omega_ref, pad, slope = refs
        else:
            arrays, refs = (refs[:6], refs[6:])
            refs = refs[:4] + refs[4 + len(earlier) :]
            top, bottom, left, right, unit_ref, base_ref, pad, slope, bend = refs
        i = pl.program_id(0) + ahead
        for f in range(count):
            trio = arrays[:3] if f < 2 else arrays[3 * (f - 1) : 3 * f]
            take = (lambda r: r[f]) if f < 2 else (lambda r: r[...])
            cur, prev, nxt = trio
            pad[f, SUB : SUB + block, LANES : LANES + cols] = take(cur)
            pad[f, 0:SUB, LANES : LANES + cols] = jnp.where(i == 0, top[f], take(prev))
            pad[f, SUB + block :, LANES : LANES + cols] = jnp.where(
                i == steps * parts - 1, bottom[f], take(nxt)
            )
            pad[f, :, 0:LANES] = left[f, pl.ds(pl.multiple_of(i * block, SUB), tall), :]
            pad[f, :, LANES + cols :] = right[f, pl.ds(pl.multiple_of(i * block, SUB), tall), :]

        def along(g, carry):
            r = pl.ds(pl.multiple_of(g * SUB, SUB), SUB)
            for f in range(count):
                for j in range(cols // wide):
                    width = wide + 2 * LANES
                    x = pad[f, r, j * wide : j * wide + width]
                    roll = lambda k: pltpu.roll(x, k % width, 1)[:, LANES : LANES + wide]
                    m2, m1, p1, p2 = roll(2), roll(1), roll(-1), roll(-2)
                    here = slice(j * wide, (j + 1) * wide)
                    slope[f, r, here] = ((m2 - p2) + 8.0 * (p1 - m1)) * (1.0 / 12.0)
                    if not want_omega:
                        mid = x[:, LANES : LANES + wide]
                        bend[f, r, here] = (16.0 * (m1 + p1) - (m2 + p2) - 30.0 * mid) * (
                            1.0 / 12.0
                        )
            return carry

        lax.fori_loop(0, tall // SUB, along, 0)

        def across(j, carry):
            inner = pl.ds(pl.multiple_of(j * chunk, LANES), chunk)
            outer = pl.ds(pl.multiple_of(j * chunk + LANES, LANES), chunk)
            for g in range(groups):
                at = lambda ref, f, k, lanes: ref[f, SUB * (g + 1) + k : SUB * (g + 2) + k, lanes]

                def first(ref, f, lanes):
                    return (
                        (at(ref, f, -2, lanes) - at(ref, f, 2, lanes))
                        + 8.0 * (at(ref, f, 1, lanes) - at(ref, f, -1, lanes))
                    ) * (1.0 / 12.0)

                ga = [first(pad, f, outer) for f in range(count)]
                gb = [at(slope, f, 0, inner) for f in range(count)]
                ta = (1.0 + ga[0], ga[1], ga[2])
                tb = (gb[0], 1.0 + gb[1], gb[2])
                n = (
                    ta[1] * tb[2] - ta[2] * tb[1],
                    ta[2] * tb[0] - ta[0] * tb[2],
                    ta[0] * tb[1] - ta[1] * tb[0],
                )
                inv = 1.0 / jnp.sqrt(n[0] * n[0] + n[1] * n[1] + n[2] * n[2])
                out = slice(g * SUB, (g + 1) * SUB)
                if want_omega:
                    omega_ref[0, 0, out, inner] = ga[3] * inv
                    omega_ref[0, 1, out, inner] = gb[3] * inv
                    continue
                unit = [v * inv for v in n]
                for f in range(3):
                    unit_ref[f, out, inner] = unit[f]
                big_e = ta[0] * ta[0] + ta[1] * ta[1] + ta[2] * ta[2]
                big_f = ta[0] * tb[0] + ta[1] * tb[1] + ta[2] * tb[2]
                big_g = tb[0] * tb[0] + tb[1] * tb[1] + tb[2] * tb[2]
                sl = sm = sn = None
                for f in range(3):
                    mid = at(pad, f, 0, outer)
                    aa = (
                        16.0 * (at(pad, f, -1, outer) + at(pad, f, 1, outer))
                        - (at(pad, f, -2, outer) + at(pad, f, 2, outer))
                        - 30.0 * mid
                    ) * (1.0 / 12.0)
                    sl = plus(sl, aa * unit[f])
                    sm = plus(sm, first(slope, f, inner) * unit[f])
                    sn = plus(sn, at(bend, f, 0, inner) * unit[f])
                curvature = (big_e * sn - 2.0 * big_f * sm + big_g * sl) * (0.5 * inv * inv)
                base_ref[out, inner] = -0.5 * at(pad, 2, 0, outer) + 0.3 * curvature
            return carry

        lax.fori_loop(0, cols // chunk, across, 0)

    per = block // SUB
    plane = [
        pl.BlockSpec((block, cols), lambda i: (i + ahead, 0)),
        pl.BlockSpec((SUB, cols), lambda i: (jnp.maximum((i + ahead) * per - 1, 0), 0)),
        pl.BlockSpec((SUB, cols), lambda i: (jnp.minimum((i + ahead + 1) * per, last), 0)),
    ]
    pair = [
        pl.BlockSpec((2, block, cols), lambda i: (0, i + ahead, 0)),
        pl.BlockSpec((2, SUB, cols), lambda i: (0, jnp.maximum((i + ahead) * per - 1, 0), 0)),
        pl.BlockSpec(
            (2, SUB, cols), lambda i: (0, jnp.minimum((i + ahead + 1) * per, last), 0)
        ),
    ]
    whole = [pl.BlockSpec(h.shape, lambda i: (0, 0, 0)) for h in halos]
    ins = [shift_plane] * 3 + [height] * 3 + ([dipole] * 3 if want_omega else [])
    scratch = [
        pltpu.VMEM((count, tall, cols + 2 * LANES), jnp.float32),
        pltpu.VMEM((count, tall, cols), jnp.float32),
    ]
    f32 = lambda *dims: jax.ShapeDtypeStruct(dims, jnp.float32)
    if want_omega:
        half = steps // tc
        out_shape = f32(tc, 2, rows // (tc * parts), cols)
        out_specs = pl.BlockSpec((1, 2, block, cols), lambda i: (i // half, 0, i % half, 0))
    else:
        out_shape = (f32(3, rows, cols), f32(rows, cols))
        out_specs = (
            pl.BlockSpec((3, block, cols), lambda i: (0, i + ahead, 0)),
            pl.BlockSpec((block, cols), lambda i: (i + ahead, 0)),
        )
        scratch.append(pltpu.VMEM((count, tall, cols), jnp.float32))
    return pl.pallas_call(
        kernel,
        grid=(steps,),
        in_specs=pair + plane * (count - 2) + whole + [pl.BlockSpec(memory_space=pl.ANY)] * len(earlier),
        out_specs=out_specs,
        out_shape=out_shape,
        scratch_shapes=scratch,
        compiler_params=params(),
        input_output_aliases={len(ins) + 4 + k: k for k in range(len(earlier))},
        name="omega" if want_omega else "geometry",
    )(*ins, *halos, *earlier)


def row_tables(outer, inner, length):
    c, s = unit_circle(outer, inner, length)
    table = np.stack([c, s]).astype(np.float32)
    return jnp.broadcast_to(jnp.asarray(table)[:, :, None, :], (2, outer, SUB, inner))


def row_forward(omega, outer, inner):
    tc, _, rows, cols = omega.shape
    kept = inner // 2
    length = tc * cols
    block = min(64, rows)
    per = outer // tc
    c, s = unit_circle(inner, kept, inner)
    matrix = two_halves(np.block([[c, -s], [s, c]]))

    def kernel(x_ref, tw_ref, m_ref, out_ref, mid):
        def step(g, carry):
            r = pl.ds(pl.multiple_of(g * SUB, SUB), SUB)
            for j in range(0, inner, LANES):
                z = []
                for l in range(outer):
                    at = (l % per) * inner + j
                    z.append((x_ref[l // per, 0, r, at : at + LANES], None))
                z = butterflies(z, 1.0)
                for n in range(outer):
                    re, im = z[n]
                    if n:
                        re, im = twist(
                            z[n],
                            tw_ref[0, n, :, j : j + LANES],
                            tw_ref[1, n, :, j : j + LANES],
                            1.0,
                        )
                    if im is None:
                        im = jnp.zeros_like(re)
                    mid[n, r, j : j + LANES] = re
                    mid[n, r, inner + j : inner + j + LANES] = im
            return carry

        lax.fori_loop(0, block // SUB, step, 0)

        def finish(n, carry):
            y = product(split(mid[n]), (m_ref[0], m_ref[1]))
            out_ref[n, 0, 0] = y[:, :kept]
            out_ref[n, 1, 0] = y[:, kept:]
            return carry

        lax.fori_loop(0, outer, finish, 0, unroll=4)

    return pl.pallas_call(
        kernel,
        grid=(2, rows // block),
        in_specs=[
            pl.BlockSpec((tc, 1, block, cols), lambda p, i: (0, p, i, 0)),
            pl.BlockSpec((2, outer, SUB, inner), lambda p, i: (0, 0, 0, 0)),
            pl.BlockSpec(matrix.shape, lambda p, i: (0, 0, 0)),
        ],
        out_specs=pl.BlockSpec((outer, 2, 1, block, kept), lambda p, i: (0, 0, p, i, 0)),
        out_shape=jax.ShapeDtypeStruct((outer, 2, 2, rows, kept), jnp.float32),
        scratch_shapes=[pltpu.VMEM((outer, block, 2 * inner), jnp.float32)],
        compiler_params=params(),
        name="rows_forward",
    )(omega, row_tables(outer, inner, length), jnp.asarray(matrix))


def column_table(outer, inner, width):
    c, s = unit_circle(outer, inner, outer * inner)
    table = jnp.asarray(np.stack([c, s]).astype(np.float32))
    return jnp.broadcast_to(table[..., None], (2, outer, inner, width))


def column_middle(spectra, table, freq_two, live_two, outer, inner):
    length = outer * inner
    parts = len(spectra)
    short, width = spectra[0].shape[-2:]
    tc = inner // short
    c, s = unit_circle(inner, inner, inner)
    matrix = two_halves(np.concatenate([c, s], 0))

    def kernel(*refs):
        x_refs, refs = (refs[:parts], refs[parts:])
        tw_ref, m_ref, f_ref, live_ref, out_ref, mid = refs

        def down(g, carry):
            r = pl.ds(pl.multiple_of(g * SUB, SUB), SUB)
            core = g // (short // SUB)
            t = pl.ds(pl.multiple_of(g % (short // SUB) * SUB, SUB), SUB)
            for p in range(2):
                z = []
                for a in range(outer):
                    ref, peer = (x_refs[a % parts], a // parts * tc + core)
                    z.append((ref[peer, 0, p, t, :], ref[peer, 1, p, t, :]))
                z = butterflies(z, 1.0)
                for k in range(outer):
                    re, im = z[k] if k == 0 else twist(z[k], tw_ref[0, k, r], tw_ref[1, k, r], 1.0)
                    mid[k, r, (2 * p) * width : (2 * p + 1) * width] = re
                    mid[k, r, (2 * p + 1) * width : (2 * p + 2) * width] = im
            return carry

        lax.fori_loop(0, inner // SUB, down, 0)
        fre_two = f_ref[...]
        live_cols = live_ref[...]
        weights = (m_ref[0], m_ref[1])

        def turn(k, carry):
            y = product(weights, split(mid[k]))
            parts = []
            for p in range(2):
                lo = slice((2 * p) * width, (2 * p + 1) * width)
                hi = slice((2 * p + 1) * width, (2 * p + 2) * width)
                parts.append((y[:inner, lo] + y[inner:, hi], y[:inner, hi] - y[inner:, lo]))
            number = k + outer * lax.broadcasted_iota(jnp.int32, (inner, width), 0)
            signed = jnp.where(number >= length // 2, number - length, number)
            fre_one = signed.astype(jnp.float32) * (1.0 / length)
            radius = jnp.sqrt(fre_one * fre_one + fre_two * fre_two)
            live = (number != length // 2) & (live_cols > 0.0) & (radius > 0.0)
            factor = jnp.where(live, 0.5 / jnp.where(live, radius, 1.0), 0.0)
            one = factor * fre_one
            two = factor * fre_two
            sum_re = one * parts[0][0] + two * parts[1][0]
            sum_im = one * parts[0][1] + two * parts[1][1]
            w = jnp.concatenate([sum_im, -sum_re], 1)
            y = product(weights, split(w))
            mid[k, :, :width] = y[:inner, :width] - y[inner:, width:]
            mid[k, :, width : 2 * width] = y[:inner, width:] + y[inner:, :width]
            return carry

        lax.fori_loop(0, outer, turn, 0)

        def up(g, carry):
            r = pl.ds(pl.multiple_of(g * SUB, SUB), SUB)
            z = []
            for k in range(outer):
                v = (mid[k, r, :width], mid[k, r, width : 2 * width])
                z.append(v if k == 0 else twist(v, tw_ref[0, k, r], tw_ref[1, k, r], -1.0))
            z = butterflies(z, -1.0)
            for a in range(outer):
                out_ref[a, 0, r, :] = z[a][0] * (1.0 / length)
                out_ref[a, 1, r, :] = z[a][1] * (1.0 / length)
            return carry

        lax.fori_loop(0, inner // SUB, up, 0)

    return pl.pallas_call(
        kernel,
        out_shape=jax.ShapeDtypeStruct((outer, 2, inner, width), jnp.float32),
        scratch_shapes=[pltpu.VMEM((outer, inner, 4 * width), jnp.float32)],
        compiler_params=params(),
        name="columns",
    )(*spectra, table, jnp.asarray(matrix), freq_two, live_two)


def row_inverse(partial, outer, inner, tc):
    _, _, rows, kept = partial.shape
    length = outer * inner
    cols = length // tc
    per = outer // tc
    block = min(64, rows)
    c, s = unit_circle(kept, inner, inner)
    matrix = two_halves(np.block([[c, s], [-s, c]]) * (2.0 / length))

    def kernel(x_ref, tw_ref, m_ref, out_ref, mid):
        lane = lax.broadcasted_iota(jnp.int32, (block, kept), 1)

        def start(n, carry):
            weight = jnp.where((lane == 0) & (n == 0), 0.5, 1.0)
            w = jnp.concatenate([x_ref[n, 0] * weight, x_ref[n, 1] * weight], 1)
            mid[n] = product(split(w), (m_ref[0], m_ref[1]))
            return carry

        lax.fori_loop(0, outer, start, 0, unroll=4)

        def step(g, carry):
            r = pl.ds(pl.multiple_of(g * SUB, SUB), SUB)
            for j in range(0, inner, LANES):
                z = []
                for n in range(outer):
                    v = (mid[n, r, j : j + LANES], mid[n, r, inner + j : inner + j + LANES])
                    if n:
                        v = twist(
                            v,
                            tw_ref[0, n, :, j : j + LANES],
                            tw_ref[1, n, :, j : j + LANES],
                            -1.0,
                        )
                    z.append(v)
                z = butterflies(z, -1.0)
                for l in range(outer):
                    at = (l % per) * inner + j
                    out_ref[l // per, r, at : at + LANES] = z[l][0]
            return carry

        lax.fori_loop(0, block // SUB, step, 0)

    return pl.pallas_call(
        kernel,
        grid=(rows // block,),
        in_specs=[
            pl.BlockSpec((outer, 2, block, kept), lambda i: (0, 0, i, 0)),
            pl.BlockSpec((2, outer, SUB, inner), lambda i: (0, 0, 0, 0)),
            pl.BlockSpec(matrix.shape, lambda i: (0, 0, 0)),
        ],
        out_specs=pl.BlockSpec((tc, block, cols), lambda i: (0, i, 0)),
        out_shape=jax.ShapeDtypeStruct((tc, rows, cols), jnp.float32),
        scratch_shapes=[pltpu.VMEM((outer, block, 2 * inner), jnp.float32)],
        compiler_params=params(),
        name="rows_inverse",
    )(partial, row_tables(outer, inner, length), jnp.asarray(matrix))


def ring(axis):
    devices = lax.axis_size(axis)
    up = [(i, (i + 1) % devices) for i in range(devices)]
    return up, [(j, i) for i, j in up]


def edges(shift_plane, height, dipole):
    fields = lambda cut: jnp.concatenate([cut(shift_plane), cut(height[None]), cut(dipole[None])], 0)
    up, down = ring("tr")
    top = lax.ppermute(fields(lambda x: x[:, -SUB:]), "tr", up)
    bottom = lax.ppermute(fields(lambda x: x[:, :SUB]), "tr", down)

    def slab(lanes):
        body = fields(lambda x: x[..., lanes])
        return jnp.concatenate([top[..., lanes], body, bottom[..., lanes]], 1)

    up, down = ring("tc")
    left = lax.ppermute(slab(slice(-LANES, None)), "tc", up)
    right = lax.ppermute(slab(slice(0, LANES)), "tc", down)
    return top, bottom, left, right


def local_kernels(shift_plane, height, dipole):
    tc = lax.axis_size("tc")
    rows, cols = height.shape
    col_outer, col_inner = factors(cols * tc)
    row_outer, row_inner = factors(rows * lax.axis_size("tr"))
    kept = col_inner // 2
    halos = edges(shift_plane, height, dipole)
    parts = rows // row_inner
    spectra = []
    charge = dipole
    for part in range(parts):
        omega = stencil(shift_plane, height, charge, halos, tc, True, part, parts)
        omega = lax.all_to_all(omega, "tc", split_axis=0, concat_axis=0, tiled=True)
        block = row_forward(omega, col_outer, col_inner)
        block, charge = lax.optimization_barrier((block, dipole))
        block = lax.all_to_all(block, ("tr", "tc"), split_axis=0, concat_axis=0, tiled=True)
        spectra.append(block)
    planes = stencil(shift_plane, height, dipole, halos, tc, False, 0, parts)
    place = lax.axis_index(("tr", "tc")) * kept + jnp.arange(kept, dtype=jnp.int32)
    freq_two, nyquist_two = wavenumbers(cols * tc, kept, place)
    live_two = jnp.where(nyquist_two, 0.0, 1.0)
    table = column_table(row_outer, row_inner, kept)
    spectra, planes, table = lax.optimization_barrier((spectra, planes, table))
    partial = column_middle(
        spectra, table, freq_two[None, :], live_two[None, :], row_outer, row_inner
    )
    for part in range(1, parts):
        planes = stencil(shift_plane, height, dipole, halos, tc, False, part, parts, planes)
    unit, base = planes
    partial = lax.all_to_all(partial, ("tr", "tc"), split_axis=0, concat_axis=0, tiled=True)
    speed = row_inverse(partial, col_outer, col_inner, tc)
    speed = lax.all_to_all(speed, "tc", split_axis=0, concat_axis=0, tiled=True)
    speed = speed.reshape(rows, cols)
    return (speed[None] * unit, base + 0.5 * speed * speed)


def fits(rows, cols, tr, tc):
    col_outer, col_inner = factors(cols * tc)
    row_outer, row_inner = factors(rows * tr)
    peers = tr * tc
    return (
        tc > 1
        and col_outer == row_outer == peers == 16
        and col_inner // 2 == LANES
        and rows // tc == row_inner
        and rows % (tc * tc * SUB) == 0
        and rows % (SUB * tc) == 0
        and col_outer % tc == 0
    )


def solution(mesh):
    in_specs = (
        P(None, ("groups", "tr"), "tc"),
        P(("groups", "tr"), "tc"),
        P(("groups", "tr"), "tc"),
    )
    out_specs = (P(None, ("groups", "tr"), "tc"), P(("groups", "tr"), "tc"))

    def chosen(shift_plane, height, dipole):
        rows, cols = height.shape
        if fits(rows, cols, lax.axis_size("tr"), lax.axis_size("tc")):
            return local_kernels(shift_plane, height, dipole)
        return local(shift_plane, height, dipole)

    return jax.shard_map(chosen, mesh=mesh, in_specs=in_specs, out_specs=out_specs, check_vma=False)
```

```python
import math

import jax
import jax.numpy as jnp
import numpy as np
from jax import lax
from jax.experimental import pallas as pl
from jax.experimental.pallas import tpu as pltpu
from jax.sharding import PartitionSpec as P

largest_wavenumber = lax.Precision.HIGHEST


def padded_2(x, sides, width):
    for axis, dim in sides:
        devices, length = (lax.axis_size(axis), x.shape[dim])
        up = [(i, (i + 1) % devices) for i in range(devices)]
        down = [(j, i) for i, j in up]
        last = lax.slice_in_dim(x, length - width, length, axis=dim)
        initial = lax.slice_in_dim(x, 0, width, axis=dim)
        before = lax.ppermute(last, axis, up)
        after = lax.ppermute(initial, axis, down)
        x = jnp.concatenate([before, x, after], axis=dim)
    return x


def rows_first(field):
    return (
        field[..., :-4, :]
        - 8.0 * field[..., 1:-3, :]
        + 8.0 * field[..., 3:-1, :]
        - field[..., 4:, :]
    ) / 12.0


def cols_first(field):
    return (
        field[..., :-4] - 8.0 * field[..., 1:-3] + 8.0 * field[..., 3:-1] - field[..., 4:]
    ) / 12.0


def rows_second(field):
    return (
        -field[..., :-4, :]
        + 16.0 * field[..., 1:-3, :]
        - 30.0 * field[..., 2:-2, :]
        + 16.0 * field[..., 3:-1, :]
        - field[..., 4:, :]
    ) / 12.0


def second_column_split(field):
    return (
        -field[..., :-4]
        + 16.0 * field[..., 1:-3]
        - 30.0 * field[..., 2:-2]
        + 16.0 * field[..., 3:-1]
        - field[..., 4:]
    ) / 12.0


def surface(grad_a, grad_b, curve_aa, curve_bb, curve_ab):
    tan_a = (1.0 + grad_a[0], grad_a[1], grad_a[2])
    tan_b = (grad_b[0], 1.0 + grad_b[1], grad_b[2])
    normal = (
        tan_a[1] * tan_b[2] - tan_a[2] * tan_b[1],
        tan_a[2] * tan_b[0] - tan_a[0] * tan_b[2],
        tan_a[0] * tan_b[1] - tan_a[1] * tan_b[0],
    )
    area_stretch_factor = jnp.sqrt(
        normal[0] * normal[0] + normal[1] * normal[1] + normal[2] * normal[2]
    )
    unit = (
        normal[0] / area_stretch_factor,
        normal[1] / area_stretch_factor,
        normal[2] / area_stretch_factor,
    )
    first_edge_term = tan_a[0] * tan_a[0] + tan_a[1] * tan_a[1] + tan_a[2] * tan_a[2]
    first_f = tan_a[0] * tan_b[0] + tan_a[1] * tan_b[1] + tan_a[2] * tan_b[2]
    first_g = tan_b[0] * tan_b[0] + tan_b[1] * tan_b[1] + tan_b[2] * tan_b[2]
    second_l = curve_aa[0] * unit[0] + curve_aa[1] * unit[1] + curve_aa[2] * unit[2]
    second_m = curve_ab[0] * unit[0] + curve_ab[1] * unit[1] + curve_ab[2] * unit[2]
    second_n = curve_bb[0] * unit[0] + curve_bb[1] * unit[1] + curve_bb[2] * unit[2]
    curvature = (first_edge_term * second_n - 2.0 * first_f * second_m + first_g * second_l) / (
        2.0 * area_stretch_factor * area_stretch_factor
    )
    omega = (grad_a[3] / area_stretch_factor, grad_b[3] / area_stretch_factor)
    return (unit, curvature, omega)


def factors(length):
    inner = min(length, 256)
    return (length // inner, inner)


def angles(count_one, count_two, modulus):
    sample_lattice = (
        jnp.arange(count_one, dtype=jnp.int32)[:, None]
        * jnp.arange(count_two, dtype=jnp.int32)[None, :]
        % modulus
    )
    theta = sample_lattice.astype(jnp.float32) * (2.0 * math.pi / modulus)
    return (jnp.cos(theta), jnp.sin(theta))


def rotation(cos_table, sin_table, sense):
    top = jnp.stack([cos_table, sense * sin_table])
    low = jnp.stack([-sense * sin_table, cos_table])
    return jnp.stack([top, low])


def twisted(sheet_portion, cos_table, sin_table, sense):
    twist_re = sheet_portion[0] * cos_table + sense * sheet_portion[1] * sin_table
    twist_im = sheet_portion[1] * cos_table - sense * sheet_portion[0] * sin_table
    return jnp.stack([twist_re, twist_im])


def forward(values, length, kept, real_input):
    outer, inner = factors(length)
    cos_outer, sin_outer = angles(outer, outer, outer)
    if real_input:
        leading = values.shape[:-1]
        sample_lattice = values.reshape(leading + (outer, inner))
        lookup_array = jnp.stack([cos_outer, -sin_outer])
        sheet_portion = jnp.einsum(
            "...lm,zln->z...nm", sample_lattice, lookup_array, precision=largest_wavenumber
        )
    else:
        leading = values.shape[1:-1]
        sample_lattice = values.reshape((2,) + leading + (outer, inner))
        sheet_portion = jnp.einsum(
            "s...ab,tsac->t...cb",
            sample_lattice,
            rotation(cos_outer, sin_outer, 1.0),
            precision=largest_wavenumber,
        )
    cos_twist, sin_twist = angles(outer, inner, length)
    sheet_portion = twisted(sheet_portion, cos_twist, sin_twist, 1.0)
    cos_inner, sin_inner = angles(inner, kept, inner)
    result = jnp.einsum(
        "s...cb,tsbd->t...cd",
        sheet_portion,
        rotation(cos_inner, sin_inner, 1.0),
        precision=largest_wavenumber,
    )
    return result.reshape((2,) + leading + (outer * kept,))


def inverse(values, length, kept, want_imag):
    outer, inner = factors(length)
    leading = values.shape[1:-1]
    sample_lattice = values.reshape((2,) + leading + (outer, kept))
    cos_inner, sin_inner = angles(kept, inner, inner)
    sheet_portion = jnp.einsum(
        "s...cd,tsdb->t...cb",
        sample_lattice,
        rotation(cos_inner, sin_inner, -1.0),
        precision=largest_wavenumber,
    )
    cos_twist, sin_twist = angles(outer, inner, length)
    sheet_portion = twisted(sheet_portion, cos_twist, sin_twist, -1.0)
    cos_outer, sin_outer = angles(outer, outer, outer)
    if want_imag:
        result = jnp.einsum(
            "s...cb,tsca->t...ab",
            sheet_portion,
            rotation(cos_outer, sin_outer, -1.0),
            precision=largest_wavenumber,
        )
        return result.reshape((2,) + leading + (length,)) / length
    lookup_array = jnp.stack([cos_outer, -sin_outer])
    result = jnp.einsum(
        "s...cb,sca->...ab", sheet_portion, lookup_array, precision=largest_wavenumber
    )
    return result.reshape(leading + (length,)) / length


def wavenumbers(length, kept, positions):
    outer, _ = factors(length)
    number = positions // kept + outer * (positions % kept)
    signed = jnp.where(number >= length // 2, number - length, number)
    return (signed.astype(jnp.float32) / length, number == length // 2)


def local(shift_plane, height, dipole):
    fields = jnp.concatenate([shift_plane, height[None], dipole[None]], 0)
    padded = padded_2(fields, (("tr", 1), ("tc", 2)), 2)
    grad_a = rows_first(padded)[..., 2:-2]
    grad_b = cols_first(padded)[..., 2:-2, :]
    curve_aa = rows_second(padded[:3])[..., 2:-2]
    curve_bb = second_column_split(padded[:3])[..., 2:-2, :]
    curve_ab = rows_first(cols_first(padded[:3]))
    unit, curvature, omega = surface(grad_a, grad_b, curve_aa, curve_bb, curve_ab)
    vorticity = jnp.stack([omega[0], omega[1]])
    sheet_rows = lax.all_to_all(vorticity, "tc", split_axis=1, concat_axis=2, tiled=True)
    col_count = sheet_rows.shape[-1]
    row_count = height.shape[0] * lax.axis_size("tr")
    col_outer, col_inner = factors(col_count)
    _, row_inner = factors(row_count)
    kept = col_inner // 2
    row_spec = forward(sheet_rows, col_count, kept, True)
    stacked = row_spec.reshape((4,) + row_spec.shape[2:])
    columns = lax.all_to_all(stacked, ("tr", "tc"), split_axis=2, concat_axis=1, tiled=True)
    columns = jnp.swapaxes(columns, 1, 2)
    local_width = columns.shape[1]
    full = forward(columns.reshape((2, 2) + columns.shape[1:]), row_count, row_inner, False)
    complete_real_part = full[0]
    full_im = full[1]
    place = lax.axis_index(("tr", "tc")) * local_width + jnp.arange(local_width, dtype=jnp.int32)
    freq_two, nyquist_two = wavenumbers(col_count, kept, place)
    freq_one, nyquist_one = wavenumbers(
        row_count, row_inner, jnp.arange(row_count, dtype=jnp.int32)
    )
    freq_one = freq_one[None, :]
    freq_two = freq_two[:, None]
    radius = jnp.sqrt(freq_one * freq_one + freq_two * freq_two)
    live = (
        jnp.logical_not(nyquist_one[None, :])
        & jnp.logical_not(nyquist_two[:, None])
        & (radius > 0.0)
    )
    factor = jnp.where(live, 0.5 / jnp.where(live, radius, 1.0), 0.0)
    summed_re = factor * (freq_one * complete_real_part[0] + freq_two * complete_real_part[1])
    summed_im = factor * (freq_one * full_im[0] + freq_two * full_im[1])
    speed_parts = inverse(jnp.stack([summed_im, -summed_re]), row_count, row_inner, True)
    partial_value = jnp.swapaxes(speed_parts, 1, 2)
    back_rows = lax.all_to_all(partial_value, ("tr", "tc"), split_axis=1, concat_axis=2, tiled=True)
    weights = (
        jnp.full((col_outer, kept), 2.0, jnp.float32).at[0, 0].set(1.0).reshape(col_outer * kept)
    )
    speed_rows = inverse(back_rows * weights, col_count, kept, False)
    speed = lax.all_to_all(speed_rows, "tc", split_axis=1, concat_axis=0, tiled=True)
    velocity_update = jnp.stack([speed * unit[0], speed * unit[1], speed * unit[2]])
    dipole_update = -2.0 * 0.5 * 0.5 * height + 0.3 * curvature + 0.5 * speed * speed
    return (velocity_update, dipole_update)


LANES = 128
SUB = 8
VMEM_BYTES = 58 * 1024 * 1024


def params():
    return pltpu.CompilerParams(vmem_limit_bytes=VMEM_BYTES)


def two_halves(table):
    table = np.asarray(table, np.float32)
    high = table.astype(jnp.bfloat16)
    low = (table - high.astype(np.float32)).astype(jnp.bfloat16)
    return np.stack([high, low])


def unit_circle(count_one, count_two, modulus):
    theta = np.arange(count_one)[:, None] * np.arange(count_two)[None, :] % modulus
    theta = theta * (2.0 * math.pi / modulus)
    return np.cos(theta), np.sin(theta)


def split(x):
    high = x.astype(jnp.bfloat16)
    low = (x - high.astype(jnp.float32)).astype(jnp.bfloat16)
    return high, low


def product(a, b):
    dot = lambda p, q: jnp.dot(p, q, preferred_element_type=jnp.float32)
    return dot(a[0], b[0]) + (dot(a[0], b[1]) + dot(a[1], b[0]))


def plus(p, q):
    return q if p is None else p if q is None else p + q


def minus(p, q):
    if q is None:
        return p
    return -q if p is None else p - q


def turned(z, number, size, sense):
    re, im = z
    number = number % size
    if number == 0:
        return z
    if 4 * number == size:
        if sense > 0:
            return (im, None if re is None else -re)
        return (None if im is None else -im, re)
    c = math.cos(2.0 * math.pi * number / size)
    s = -sense * math.sin(2.0 * math.pi * number / size)
    if 8 * number == size:
        r = math.sqrt(0.5)
        if im is None:
            return (re * r, re * (-sense * r))
        if sense > 0:
            return ((re + im) * r, (im - re) * r)
        return ((re - im) * r, (im + re) * r)
    if im is None:
        return (re * c, re * s)
    return (re * c - im * s, re * s + im * c)


def butterflies(z, sense):
    size = len(z)
    if size == 1:
        return z
    even = butterflies(z[0::2], sense)
    odd = butterflies(z[1::2], sense)
    odd = [turned(o, k, size, sense) for k, o in enumerate(odd)]
    head = [(plus(e[0], o[0]), plus(e[1], o[1])) for e, o in zip(even, odd)]
    tail = [(minus(e[0], o[0]), minus(e[1], o[1])) for e, o in zip(even, odd)]
    return head + tail


def twist(z, c, s, sense):
    re, im = z
    if im is None:
        return (re * c, re * s * (-sense))
    if sense > 0:
        return (re * c + im * s, im * c - re * s)
    return (re * c - im * s, im * c + re * s)


def stencil(shift_plane, height, dipole, halos, tc, want_omega, part, parts, earlier=()):
    rows, cols = height.shape
    block = min(64, rows // (tc * parts))
    steps = rows // (block * parts)
    ahead = part * steps
    chunk = min(128, cols)
    wide = min(1024, cols)
    groups = block // SUB
    count = 4 if want_omega else 3
    tall = block + 2 * SUB
    last = rows // SUB - 1

    def kernel(*refs):
        if want_omega:
            arrays, refs = (refs[:9], refs[9:])
            top, bottom, left, right, omega_ref, pad, slope = refs
        else:
            arrays, refs = (refs[:6], refs[6:])
            refs = refs[:4] + refs[4 + len(earlier) :]
            top, bottom, left, right, unit_ref, base_ref, pad, slope, bend = refs
        i = pl.program_id(0) + ahead
        for f in range(count):
            trio = arrays[:3] if f < 2 else arrays[3 * (f - 1) : 3 * f]
            take = (lambda r: r[f]) if f < 2 else (lambda r: r[...])
            cur, prev, nxt = trio
            pad[f, SUB : SUB + block, LANES : LANES + cols] = take(cur)
            pad[f, 0:SUB, LANES : LANES + cols] = jnp.where(i == 0, top[f], take(prev))
            pad[f, SUB + block :, LANES : LANES + cols] = jnp.where(
                i == steps * parts - 1, bottom[f], take(nxt)
            )
            pad[f, :, 0:LANES] = left[f, pl.ds(pl.multiple_of(i * block, SUB), tall), :]
            pad[f, :, LANES + cols :] = right[f, pl.ds(pl.multiple_of(i * block, SUB), tall), :]

        def along(g, carry):
            r = pl.ds(pl.multiple_of(g * SUB, SUB), SUB)
            for f in range(count):
                for j in range(cols // wide):
                    width = wide + 2 * LANES
                    x = pad[f, r, j * wide : j * wide + width]
                    roll = lambda k: pltpu.roll(x, k % width, 1)[:, LANES : LANES + wide]
                    m2, m1, p1, p2 = roll(2), roll(1), roll(-1), roll(-2)
                    here = slice(j * wide, (j + 1) * wide)
                    slope[f, r, here] = ((m2 - p2) + 8.0 * (p1 - m1)) * (1.0 / 12.0)
                    if not want_omega:
                        mid = x[:, LANES : LANES + wide]
                        bend[f, r, here] = (16.0 * (m1 + p1) - (m2 + p2) - 30.0 * mid) * (
                            1.0 / 12.0
                        )
            return carry

        lax.fori_loop(0, tall // SUB, along, 0)

        def across(j, carry):
            inner = pl.ds(pl.multiple_of(j * chunk, LANES), chunk)
            outer = pl.ds(pl.multiple_of(j * chunk + LANES, LANES), chunk)
            for g in range(groups):
                at = lambda ref, f, k, lanes: ref[f, SUB * (g + 1) + k : SUB * (g + 2) + k, lanes]

                def first(ref, f, lanes):
                    return (
                        (at(ref, f, -2, lanes) - at(ref, f, 2, lanes))
                        + 8.0 * (at(ref, f, 1, lanes) - at(ref, f, -1, lanes))
                    ) * (1.0 / 12.0)

                ga = [first(pad, f, outer) for f in range(count)]
                gb = [at(slope, f, 0, inner) for f in range(count)]
                ta = (1.0 + ga[0], ga[1], ga[2])
                tb = (gb[0], 1.0 + gb[1], gb[2])
                n = (
                    ta[1] * tb[2] - ta[2] * tb[1],
                    ta[2] * tb[0] - ta[0] * tb[2],
                    ta[0] * tb[1] - ta[1] * tb[0],
                )
                inv = 1.0 / jnp.sqrt(n[0] * n[0] + n[1] * n[1] + n[2] * n[2])
                out = slice(g * SUB, (g + 1) * SUB)
                if want_omega:
                    omega_ref[0, 0, out, inner] = ga[3] * inv
                    omega_ref[0, 1, out, inner] = gb[3] * inv
                    continue
                unit = [v * inv for v in n]
                for f in range(3):
                    unit_ref[f, out, inner] = unit[f]
                big_e = ta[0] * ta[0] + ta[1] * ta[1] + ta[2] * ta[2]
                big_f = ta[0] * tb[0] + ta[1] * tb[1] + ta[2] * tb[2]
                big_g = tb[0] * tb[0] + tb[1] * tb[1] + tb[2] * tb[2]
                sl = sm = sn = None
                for f in range(3):
                    mid = at(pad, f, 0, outer)
                    aa = (
                        16.0 * (at(pad, f, -1, outer) + at(pad, f, 1, outer))
                        - (at(pad, f, -2, outer) + at(pad, f, 2, outer))
                        - 30.0 * mid
                    ) * (1.0 / 12.0)
                    sl = plus(sl, aa * unit[f])
                    sm = plus(sm, first(slope, f, inner) * unit[f])
                    sn = plus(sn, at(bend, f, 0, inner) * unit[f])
                curvature = (big_e * sn - 2.0 * big_f * sm + big_g * sl) * (0.5 * inv * inv)
                base_ref[out, inner] = -0.5 * at(pad, 2, 0, outer) + 0.3 * curvature
            return carry

        lax.fori_loop(0, cols // chunk, across, 0)

    per = block // SUB
    plane = [
        pl.BlockSpec((block, cols), lambda i: (i + ahead, 0)),
        pl.BlockSpec((SUB, cols), lambda i: (jnp.maximum((i + ahead) * per - 1, 0), 0)),
        pl.BlockSpec((SUB, cols), lambda i: (jnp.minimum((i + ahead + 1) * per, last), 0)),
    ]
    pair = [
        pl.BlockSpec((2, block, cols), lambda i: (0, i + ahead, 0)),
        pl.BlockSpec((2, SUB, cols), lambda i: (0, jnp.maximum((i + ahead) * per - 1, 0), 0)),
        pl.BlockSpec(
            (2, SUB, cols), lambda i: (0, jnp.minimum((i + ahead + 1) * per, last), 0)
        ),
    ]
    whole = [pl.BlockSpec(h.shape, lambda i: (0, 0, 0)) for h in halos]
    ins = [shift_plane] * 3 + [height] * 3 + ([dipole] * 3 if want_omega else [])
    scratch = [
        pltpu.VMEM((count, tall, cols + 2 * LANES), jnp.float32),
        pltpu.VMEM((count, tall, cols), jnp.float32),
    ]
    f32 = lambda *dims: jax.ShapeDtypeStruct(dims, jnp.float32)
    if want_omega:
        half = steps // tc
        out_shape = f32(tc, 2, rows // (tc * parts), cols)
        out_specs = pl.BlockSpec((1, 2, block, cols), lambda i: (i // half, 0, i % half, 0))
    else:
        out_shape = (f32(3, rows, cols), f32(rows, cols))
        out_specs = (
            pl.BlockSpec((3, block, cols), lambda i: (0, i + ahead, 0)),
            pl.BlockSpec((block, cols), lambda i: (i + ahead, 0)),
        )
        scratch.append(pltpu.VMEM((count, tall, cols), jnp.float32))
    return pl.pallas_call(
        kernel,
        grid=(steps,),
        in_specs=pair + plane * (count - 2) + whole + [pl.BlockSpec(memory_space=pl.ANY)] * len(earlier),
        out_specs=out_specs,
        out_shape=out_shape,
        scratch_shapes=scratch,
        compiler_params=params(),
        input_output_aliases={len(ins) + 4 + k: k for k in range(len(earlier))},
        name="omega" if want_omega else "geometry",
    )(*ins, *halos, *earlier)


def row_tables(outer, inner, length):
    c, s = unit_circle(outer, inner, length)
    table = np.stack([c, s]).astype(np.float32)
    return jnp.broadcast_to(jnp.asarray(table)[:, :, None, :], (2, outer, SUB, inner))


def row_forward(omega, outer, inner):
    tc, _, rows, cols = omega.shape
    kept = inner // 2
    length = tc * cols
    block = min(64, rows)
    per = outer // tc
    c, s = unit_circle(inner, kept, inner)
    matrix = two_halves(np.block([[c, -s], [s, c]]))

    def kernel(x_ref, tw_ref, m_ref, out_ref, mid):
        def step(g, carry):
            r = pl.ds(pl.multiple_of(g * SUB, SUB), SUB)
            for j in range(0, inner, LANES):
                z = []
                for l in range(outer):
                    at = (l % per) * inner + j
                    z.append((x_ref[l // per, 0, r, at : at + LANES], None))
                z = butterflies(z, 1.0)
                for n in range(outer):
                    re, im = z[n]
                    if n:
                        re, im = twist(
                            z[n],
                            tw_ref[0, n, :, j : j + LANES],
                            tw_ref[1, n, :, j : j + LANES],
                            1.0,
                        )
                    if im is None:
                        im = jnp.zeros_like(re)
                    mid[n, r, j : j + LANES] = re
                    mid[n, r, inner + j : inner + j + LANES] = im
            return carry

        lax.fori_loop(0, block // SUB, step, 0)

        def finish(n, carry):
            y = product(split(mid[n]), (m_ref[0], m_ref[1]))
            out_ref[n, 0, 0] = y[:, :kept]
            out_ref[n, 1, 0] = y[:, kept:]
            return carry

        lax.fori_loop(0, outer, finish, 0, unroll=4)

    return pl.pallas_call(
        kernel,
        grid=(2, rows // block),
        in_specs=[
            pl.BlockSpec((tc, 1, block, cols), lambda p, i: (0, p, i, 0)),
            pl.BlockSpec((2, outer, SUB, inner), lambda p, i: (0, 0, 0, 0)),
            pl.BlockSpec(matrix.shape, lambda p, i: (0, 0, 0)),
        ],
        out_specs=pl.BlockSpec((outer, 2, 1, block, kept), lambda p, i: (0, 0, p, i, 0)),
        out_shape=jax.ShapeDtypeStruct((outer, 2, 2, rows, kept), jnp.float32),
        scratch_shapes=[pltpu.VMEM((outer, block, 2 * inner), jnp.float32)],
        compiler_params=params(),
        name="rows_forward",
    )(omega, row_tables(outer, inner, length), jnp.asarray(matrix))


def column_table(outer, inner, width):
    c, s = unit_circle(outer, inner, outer * inner)
    table = jnp.asarray(np.stack([c, s]).astype(np.float32))
    return jnp.broadcast_to(table[..., None], (2, outer, inner, width))


def column_middle(spectra, table, freq_two, live_two, outer, inner):
    length = outer * inner
    parts = len(spectra)
    short, width = spectra[0].shape[-2:]
    tc = inner // short
    c, s = unit_circle(inner, inner, inner)
    matrix = two_halves(np.concatenate([c, s], 0))

    def kernel(*refs):
        x_refs, refs = (refs[:parts], refs[parts:])
        tw_ref, m_ref, f_ref, live_ref = refs[:4]
        out_refs, mid = (refs[4:-1], refs[-1])

        def down(g, carry):
            r = pl.ds(pl.multiple_of(g * SUB, SUB), SUB)
            core = g // (short // SUB)
            t = pl.ds(pl.multiple_of(g % (short // SUB) * SUB, SUB), SUB)
            for p in range(2):
                z = []
                for a in range(outer):
                    ref, peer = (x_refs[a % parts], a // parts * tc + core)
                    z.append((ref[peer, 0, p, t, :], ref[peer, 1, p, t, :]))
                z = butterflies(z, 1.0)
                for k in range(outer):
                    re, im = z[k] if k == 0 else twist(z[k], tw_ref[0, k, r], tw_ref[1, k, r], 1.0)
                    mid[k, r, (2 * p) * width : (2 * p + 1) * width] = re
                    mid[k, r, (2 * p + 1) * width : (2 * p + 2) * width] = im
            return carry

        lax.fori_loop(0, inner // SUB, down, 0)
        fre_two = f_ref[...]
        live_cols = live_ref[...]
        weights = (m_ref[0], m_ref[1])

        def turn(k, carry):
            y = product(weights, split(mid[k]))
            parts = []
            for p in range(2):
                lo = slice((2 * p) * width, (2 * p + 1) * width)
                hi = slice((2 * p + 1) * width, (2 * p + 2) * width)
                parts.append((y[:inner, lo] + y[inner:, hi], y[:inner, hi] - y[inner:, lo]))
            number = k + outer * lax.broadcasted_iota(jnp.int32, (inner, width), 0)
            signed = jnp.where(number >= length // 2, number - length, number)
            fre_one = signed.astype(jnp.float32) * (1.0 / length)
            radius = jnp.sqrt(fre_one * fre_one + fre_two * fre_two)
            live = (number != length // 2) & (live_cols > 0.0) & (radius > 0.0)
            factor = jnp.where(live, 0.5 / jnp.where(live, radius, 1.0), 0.0)
            one = factor * fre_one
            two = factor * fre_two
            sum_re = one * parts[0][0] + two * parts[1][0]
            sum_im = one * parts[0][1] + two * parts[1][1]
            w = jnp.concatenate([sum_im, -sum_re], 1)
            y = product(weights, split(w))
            mid[k, :, :width] = y[:inner, :width] - y[inner:, width:]
            mid[k, :, width : 2 * width] = y[:inner, width:] + y[inner:, :width]
            return carry

        lax.fori_loop(0, outer, turn, 0)

        for h, out_ref in enumerate(out_refs):

            def up(g, carry):
                r = pl.ds(pl.multiple_of(g * SUB + h * length // outer // parts, SUB), SUB)
                t = pl.ds(pl.multiple_of(g * SUB, SUB), SUB)
                z = []
                for k in range(outer):
                    v = (mid[k, r, :width], mid[k, r, width : 2 * width])
                    z.append(v if k == 0 else twist(v, tw_ref[0, k, r], tw_ref[1, k, r], -1.0))
                z = butterflies(z, -1.0)
                for a in range(outer):
                    out_ref[a, 0, t, :] = z[a][0] * (1.0 / length)
                    out_ref[a, 1, t, :] = z[a][1] * (1.0 / length)
                return carry

            lax.fori_loop(0, inner // parts // SUB, up, 0)

    return pl.pallas_call(
        kernel,
        out_shape=[jax.ShapeDtypeStruct((outer, 2, inner // parts, width), jnp.float32)] * parts,
        scratch_shapes=[pltpu.VMEM((outer, inner, 4 * width), jnp.float32)],
        compiler_params=params(),
        name="columns",
    )(*spectra, table, jnp.asarray(matrix), freq_two, live_two)


def row_inverse(partial, outer, inner, tc):
    _, _, rows, kept = partial.shape
    length = outer * inner
    cols = length // tc
    per = outer // tc
    block = min(64, rows)
    c, s = unit_circle(kept, inner, inner)
    matrix = two_halves(np.block([[c, s], [-s, c]]) * (2.0 / length))

    def kernel(x_ref, tw_ref, m_ref, out_ref, mid):
        lane = lax.broadcasted_iota(jnp.int32, (block, kept), 1)

        def start(n, carry):
            weight = jnp.where((lane == 0) & (n == 0), 0.5, 1.0)
            w = jnp.concatenate([x_ref[n, 0] * weight, x_ref[n, 1] * weight], 1)
            mid[n] = product(split(w), (m_ref[0], m_ref[1]))
            return carry

        lax.fori_loop(0, outer, start, 0, unroll=4)

        def step(g, carry):
            r = pl.ds(pl.multiple_of(g * SUB, SUB), SUB)
            for j in range(0, inner, LANES):
                z = []
                for n in range(outer):
                    v = (mid[n, r, j : j + LANES], mid[n, r, inner + j : inner + j + LANES])
                    if n:
                        v = twist(
                            v,
                            tw_ref[0, n, :, j : j + LANES],
                            tw_ref[1, n, :, j : j + LANES],
                            -1.0,
                        )
                    z.append(v)
                z = butterflies(z, -1.0)
                for l in range(outer):
                    at = (l % per) * inner + j
                    out_ref[l // per, r, at : at + LANES] = z[l][0]
            return carry

        lax.fori_loop(0, block // SUB, step, 0)

    return pl.pallas_call(
        kernel,
        grid=(rows // block,),
        in_specs=[
            pl.BlockSpec((outer, 2, block, kept), lambda i: (0, 0, i, 0)),
            pl.BlockSpec((2, outer, SUB, inner), lambda i: (0, 0, 0, 0)),
            pl.BlockSpec(matrix.shape, lambda i: (0, 0, 0)),
        ],
        out_specs=pl.BlockSpec((tc, block, cols), lambda i: (0, i, 0)),
        out_shape=jax.ShapeDtypeStruct((tc, rows, cols), jnp.float32),
        scratch_shapes=[pltpu.VMEM((outer, block, 2 * inner), jnp.float32)],
        compiler_params=params(),
        name="rows_inverse",
    )(partial, row_tables(outer, inner, length), jnp.asarray(matrix))


def ring(axis):
    devices = lax.axis_size(axis)
    up = [(i, (i + 1) % devices) for i in range(devices)]
    return up, [(j, i) for i, j in up]


def edges(shift_plane, height, dipole):
    fields = lambda cut: jnp.concatenate([cut(shift_plane), cut(height[None]), cut(dipole[None])], 0)
    up, down = ring("tr")
    top = lax.ppermute(fields(lambda x: x[:, -SUB:]), "tr", up)
    bottom = lax.ppermute(fields(lambda x: x[:, :SUB]), "tr", down)

    def slab(lanes):
        body = fields(lambda x: x[..., lanes])
        return jnp.concatenate([top[..., lanes], body, bottom[..., lanes]], 1)

    up, down = ring("tc")
    left = lax.ppermute(slab(slice(-LANES, None)), "tc", up)
    right = lax.ppermute(slab(slice(0, LANES)), "tc", down)
    return top, bottom, left, right


def exchange(x, covered):
    if not covered:
        return lax.all_to_all(x, "tc", split_axis=0, concat_axis=0, tiled=True)
    other = 1 - lax.axis_index("tc")
    sent = lax.dynamic_index_in_dim(x, other, 0, keepdims=True)
    got = lax.ppermute(sent, "tc", ring("tc")[0])
    return lax.dynamic_update_slice_in_dim(x, got, other, 0)


def local_kernels(shift_plane, height, dipole):
    tc = lax.axis_size("tc")
    rows, cols = height.shape
    col_outer, col_inner = factors(cols * tc)
    row_outer, row_inner = factors(rows * lax.axis_size("tr"))
    kept = col_inner // 2
    halos = edges(shift_plane, height, dipole)
    parts = rows // row_inner
    spectra = []
    charge = dipole
    for part in range(parts):
        omega = stencil(shift_plane, height, charge, halos, tc, True, part, parts)
        omega = exchange(omega, part > 0)
        block = row_forward(omega, col_outer, col_inner)
        block, charge = lax.optimization_barrier((block, dipole))
        block = lax.all_to_all(block, ("tr", "tc"), split_axis=0, concat_axis=0, tiled=True)
        spectra.append(block)
    planes = stencil(shift_plane, height, dipole, halos, tc, False, 0, parts)
    place = lax.axis_index(("tr", "tc")) * kept + jnp.arange(kept, dtype=jnp.int32)
    freq_two, nyquist_two = wavenumbers(cols * tc, kept, place)
    live_two = jnp.where(nyquist_two, 0.0, 1.0)
    table = column_table(row_outer, row_inner, kept)
    spectra, planes, table = lax.optimization_barrier((spectra, planes, table))
    partial = column_middle(
        spectra, table, freq_two[None, :], live_two[None, :], row_outer, row_inner
    )
    for part in range(1, parts):
        planes = stencil(shift_plane, height, dipole, halos, tc, False, part, parts, planes)
    unit, base = planes
    results = ()
    for part in range(parts):
        block = lax.all_to_all(partial[part], ("tr", "tc"), split_axis=0, concat_axis=0, tiled=True)
        speed = row_inverse(block, col_outer, col_inner, tc)
        speed = exchange(speed, part < parts - 1)
        results = finish(speed, unit, base, part, parts, results)
    return tuple(results)


def finish(speed, unit, base, part, parts, earlier):
    _, cols = base.shape
    tc, short, _ = speed.shape
    block = min(64, short)
    steps = short // block

    def kernel(s_ref, u_ref, b_ref, *refs):
        v_ref, d_ref = refs[len(earlier) :]
        s = s_ref[0]
        for f in range(3):
            v_ref[f] = s * u_ref[f]
        d_ref[...] = b_ref[...] + 0.5 * s * s

    row = lambda t, j: (t * parts + part) * steps + j
    plane = pl.BlockSpec((block, cols), lambda t, j: (row(t, j), 0))
    triple = pl.BlockSpec((3, block, cols), lambda t, j: (0, row(t, j), 0))
    return pl.pallas_call(
        kernel,
        grid=(tc, steps),
        in_specs=[pl.BlockSpec((1, block, cols), lambda t, j: (t, j, 0)), triple, plane]
        + [pl.BlockSpec(memory_space=pl.ANY)] * len(earlier),
        out_specs=(triple, plane),
        out_shape=(
            jax.ShapeDtypeStruct(unit.shape, jnp.float32),
            jax.ShapeDtypeStruct(base.shape, jnp.float32),
        ),
        input_output_aliases={3 + k: k for k in range(len(earlier))},
        compiler_params=params(),
        name="finish",
    )(speed, unit, base, *earlier)


def fits(rows, cols, tr, tc):
    col_outer, col_inner = factors(cols * tc)
    row_outer, row_inner = factors(rows * tr)
    peers = tr * tc
    return (
        tc == 2
        and col_outer == row_outer == peers == 16
        and col_inner // 2 == LANES
        and rows // tc == row_inner
        and rows % (tc * tc * SUB) == 0
        and rows % (SUB * tc) == 0
        and col_outer % tc == 0
    )


def solution(mesh):
    in_specs = (
        P(None, ("groups", "tr"), "tc"),
        P(("groups", "tr"), "tc"),
        P(("groups", "tr"), "tc"),
    )
    out_specs = (P(None, ("groups", "tr"), "tc"), P(("groups", "tr"), "tc"))

    def chosen(shift_plane, height, dipole):
        rows, cols = height.shape
        if fits(rows, cols, lax.axis_size("tr"), lax.axis_size("tc")):
            return local_kernels(shift_plane, height, dipole)
        return local(shift_plane, height, dipole)

    return jax.shard_map(
        chosen, mesh=mesh, in_specs=in_specs, out_specs=out_specs, check_vma=False
    )
```

```python
import math

import jax
import jax.numpy as jnp
import numpy as np
from jax import lax
from jax.experimental import pallas as pl
from jax.experimental.pallas import tpu as pltpu
from jax.sharding import PartitionSpec as P

largest_wavenumber = lax.Precision.HIGHEST


def padded_2(x, sides, width):
    for axis, dim in sides:
        devices, length = (lax.axis_size(axis), x.shape[dim])
        up = [(i, (i + 1) % devices) for i in range(devices)]
        down = [(j, i) for i, j in up]
        last = lax.slice_in_dim(x, length - width, length, axis=dim)
        initial = lax.slice_in_dim(x, 0, width, axis=dim)
        before = lax.ppermute(last, axis, up)
        after = lax.ppermute(initial, axis, down)
        x = jnp.concatenate([before, x, after], axis=dim)
    return x


def rows_first(field):
    return (
        field[..., :-4, :]
        - 8.0 * field[..., 1:-3, :]
        + 8.0 * field[..., 3:-1, :]
        - field[..., 4:, :]
    ) / 12.0


def cols_first(field):
    return (
        field[..., :-4] - 8.0 * field[..., 1:-3] + 8.0 * field[..., 3:-1] - field[..., 4:]
    ) / 12.0


def rows_second(field):
    return (
        -field[..., :-4, :]
        + 16.0 * field[..., 1:-3, :]
        - 30.0 * field[..., 2:-2, :]
        + 16.0 * field[..., 3:-1, :]
        - field[..., 4:, :]
    ) / 12.0


def second_column_split(field):
    return (
        -field[..., :-4]
        + 16.0 * field[..., 1:-3]
        - 30.0 * field[..., 2:-2]
        + 16.0 * field[..., 3:-1]
        - field[..., 4:]
    ) / 12.0


def surface(grad_a, grad_b, curve_aa, curve_bb, curve_ab):
    tan_a = (1.0 + grad_a[0], grad_a[1], grad_a[2])
    tan_b = (grad_b[0], 1.0 + grad_b[1], grad_b[2])
    normal = (
        tan_a[1] * tan_b[2] - tan_a[2] * tan_b[1],
        tan_a[2] * tan_b[0] - tan_a[0] * tan_b[2],
        tan_a[0] * tan_b[1] - tan_a[1] * tan_b[0],
    )
    area_stretch_factor = jnp.sqrt(
        normal[0] * normal[0] + normal[1] * normal[1] + normal[2] * normal[2]
    )
    unit = (
        normal[0] / area_stretch_factor,
        normal[1] / area_stretch_factor,
        normal[2] / area_stretch_factor,
    )
    first_edge_term = tan_a[0] * tan_a[0] + tan_a[1] * tan_a[1] + tan_a[2] * tan_a[2]
    first_f = tan_a[0] * tan_b[0] + tan_a[1] * tan_b[1] + tan_a[2] * tan_b[2]
    first_g = tan_b[0] * tan_b[0] + tan_b[1] * tan_b[1] + tan_b[2] * tan_b[2]
    second_l = curve_aa[0] * unit[0] + curve_aa[1] * unit[1] + curve_aa[2] * unit[2]
    second_m = curve_ab[0] * unit[0] + curve_ab[1] * unit[1] + curve_ab[2] * unit[2]
    second_n = curve_bb[0] * unit[0] + curve_bb[1] * unit[1] + curve_bb[2] * unit[2]
    curvature = (first_edge_term * second_n - 2.0 * first_f * second_m + first_g * second_l) / (
        2.0 * area_stretch_factor * area_stretch_factor
    )
    omega = (grad_a[3] / area_stretch_factor, grad_b[3] / area_stretch_factor)
    return (unit, curvature, omega)


def factors(length):
    inner = min(length, 256)
    return (length // inner, inner)


def angles(count_one, count_two, modulus):
    sample_lattice = (
        jnp.arange(count_one, dtype=jnp.int32)[:, None]
        * jnp.arange(count_two, dtype=jnp.int32)[None, :]
        % modulus
    )
    theta = sample_lattice.astype(jnp.float32) * (2.0 * math.pi / modulus)
    return (jnp.cos(theta), jnp.sin(theta))


def rotation(cos_table, sin_table, sense):
    top = jnp.stack([cos_table, sense * sin_table])
    low = jnp.stack([-sense * sin_table, cos_table])
    return jnp.stack([top, low])


def twisted(sheet_portion, cos_table, sin_table, sense):
    twist_re = sheet_portion[0] * cos_table + sense * sheet_portion[1] * sin_table
    twist_im = sheet_portion[1] * cos_table - sense * sheet_portion[0] * sin_table
    return jnp.stack([twist_re, twist_im])


def forward(values, length, kept, real_input):
    outer, inner = factors(length)
    cos_outer, sin_outer = angles(outer, outer, outer)
    if real_input:
        leading = values.shape[:-1]
        sample_lattice = values.reshape(leading + (outer, inner))
        lookup_array = jnp.stack([cos_outer, -sin_outer])
        sheet_portion = jnp.einsum(
            "...lm,zln->z...nm", sample_lattice, lookup_array, precision=largest_wavenumber
        )
    else:
        leading = values.shape[1:-1]
        sample_lattice = values.reshape((2,) + leading + (outer, inner))
        sheet_portion = jnp.einsum(
            "s...ab,tsac->t...cb",
            sample_lattice,
            rotation(cos_outer, sin_outer, 1.0),
            precision=largest_wavenumber,
        )
    cos_twist, sin_twist = angles(outer, inner, length)
    sheet_portion = twisted(sheet_portion, cos_twist, sin_twist, 1.0)
    cos_inner, sin_inner = angles(inner, kept, inner)
    result = jnp.einsum(
        "s...cb,tsbd->t...cd",
        sheet_portion,
        rotation(cos_inner, sin_inner, 1.0),
        precision=largest_wavenumber,
    )
    return result.reshape((2,) + leading + (outer * kept,))


def inverse(values, length, kept, want_imag):
    outer, inner = factors(length)
    leading = values.shape[1:-1]
    sample_lattice = values.reshape((2,) + leading + (outer, kept))
    cos_inner, sin_inner = angles(kept, inner, inner)
    sheet_portion = jnp.einsum(
        "s...cd,tsdb->t...cb",
        sample_lattice,
        rotation(cos_inner, sin_inner, -1.0),
        precision=largest_wavenumber,
    )
    cos_twist, sin_twist = angles(outer, inner, length)
    sheet_portion = twisted(sheet_portion, cos_twist, sin_twist, -1.0)
    cos_outer, sin_outer = angles(outer, outer, outer)
    if want_imag:
        result = jnp.einsum(
            "s...cb,tsca->t...ab",
            sheet_portion,
            rotation(cos_outer, sin_outer, -1.0),
            precision=largest_wavenumber,
        )
        return result.reshape((2,) + leading + (length,)) / length
    lookup_array = jnp.stack([cos_outer, -sin_outer])
    result = jnp.einsum(
        "s...cb,sca->...ab", sheet_portion, lookup_array, precision=largest_wavenumber
    )
    return result.reshape(leading + (length,)) / length


def wavenumbers(length, kept, positions):
    outer, _ = factors(length)
    number = positions // kept + outer * (positions % kept)
    signed = jnp.where(number >= length // 2, number - length, number)
    return (signed.astype(jnp.float32) / length, number == length // 2)


def local(shift_plane, height, dipole):
    fields = jnp.concatenate([shift_plane, height[None], dipole[None]], 0)
    padded = padded_2(fields, (("tr", 1), ("tc", 2)), 2)
    grad_a = rows_first(padded)[..., 2:-2]
    grad_b = cols_first(padded)[..., 2:-2, :]
    curve_aa = rows_second(padded[:3])[..., 2:-2]
    curve_bb = second_column_split(padded[:3])[..., 2:-2, :]
    curve_ab = rows_first(cols_first(padded[:3]))
    unit, curvature, omega = surface(grad_a, grad_b, curve_aa, curve_bb, curve_ab)
    vorticity = jnp.stack([omega[0], omega[1]])
    sheet_rows = lax.all_to_all(vorticity, "tc", split_axis=1, concat_axis=2, tiled=True)
    col_count = sheet_rows.shape[-1]
    row_count = height.shape[0] * lax.axis_size("tr")
    col_outer, col_inner = factors(col_count)
    _, row_inner = factors(row_count)
    kept = col_inner // 2
    row_spec = forward(sheet_rows, col_count, kept, True)
    stacked = row_spec.reshape((4,) + row_spec.shape[2:])
    columns = lax.all_to_all(stacked, ("tr", "tc"), split_axis=2, concat_axis=1, tiled=True)
    columns = jnp.swapaxes(columns, 1, 2)
    local_width = columns.shape[1]
    full = forward(columns.reshape((2, 2) + columns.shape[1:]), row_count, row_inner, False)
    complete_real_part = full[0]
    full_im = full[1]
    place = lax.axis_index(("tr", "tc")) * local_width + jnp.arange(local_width, dtype=jnp.int32)
    freq_two, nyquist_two = wavenumbers(col_count, kept, place)
    freq_one, nyquist_one = wavenumbers(
        row_count, row_inner, jnp.arange(row_count, dtype=jnp.int32)
    )
    freq_one = freq_one[None, :]
    freq_two = freq_two[:, None]
    radius = jnp.sqrt(freq_one * freq_one + freq_two * freq_two)
    live = (
        jnp.logical_not(nyquist_one[None, :])
        & jnp.logical_not(nyquist_two[:, None])
        & (radius > 0.0)
    )
    factor = jnp.where(live, 0.5 / jnp.where(live, radius, 1.0), 0.0)
    summed_re = factor * (freq_one * complete_real_part[0] + freq_two * complete_real_part[1])
    summed_im = factor * (freq_one * full_im[0] + freq_two * full_im[1])
    speed_parts = inverse(jnp.stack([summed_im, -summed_re]), row_count, row_inner, True)
    partial_value = jnp.swapaxes(speed_parts, 1, 2)
    back_rows = lax.all_to_all(partial_value, ("tr", "tc"), split_axis=1, concat_axis=2, tiled=True)
    weights = (
        jnp.full((col_outer, kept), 2.0, jnp.float32).at[0, 0].set(1.0).reshape(col_outer * kept)
    )
    speed_rows = inverse(back_rows * weights, col_count, kept, False)
    speed = lax.all_to_all(speed_rows, "tc", split_axis=1, concat_axis=0, tiled=True)
    velocity_update = jnp.stack([speed * unit[0], speed * unit[1], speed * unit[2]])
    dipole_update = -2.0 * 0.5 * 0.5 * height + 0.3 * curvature + 0.5 * speed * speed
    return (velocity_update, dipole_update)


LANES = 128
SUB = 8
VMEM_BYTES = 58 * 1024 * 1024


def params():
    return pltpu.CompilerParams(vmem_limit_bytes=VMEM_BYTES)


def two_halves(table):
    table = np.asarray(table, np.float32)
    high = table.astype(jnp.bfloat16)
    low = (table - high.astype(np.float32)).astype(jnp.bfloat16)
    return np.stack([high, low])


def unit_circle(count_one, count_two, modulus):
    theta = np.arange(count_one)[:, None] * np.arange(count_two)[None, :] % modulus
    theta = theta * (2.0 * math.pi / modulus)
    return np.cos(theta), np.sin(theta)


def split(x):
    high = x.astype(jnp.bfloat16)
    low = (x - high.astype(jnp.float32)).astype(jnp.bfloat16)
    return high, low


def product(a, b):
    dot = lambda p, q: jnp.dot(p, q, preferred_element_type=jnp.float32)
    return dot(a[0], b[0]) + (dot(a[0], b[1]) + dot(a[1], b[0]))


def plus(p, q):
    return q if p is None else p if q is None else p + q


def minus(p, q):
    if q is None:
        return p
    return -q if p is None else p - q


def turned(z, number, size, sense):
    re, im = z
    number = number % size
    if number == 0:
        return z
    if 4 * number == size:
        if sense > 0:
            return (im, None if re is None else -re)
        return (None if im is None else -im, re)
    c = math.cos(2.0 * math.pi * number / size)
    s = -sense * math.sin(2.0 * math.pi * number / size)
    if 8 * number == size:
        r = math.sqrt(0.5)
        if im is None:
            return (re * r, re * (-sense * r))
        if sense > 0:
            return ((re + im) * r, (im - re) * r)
        return ((re - im) * r, (im + re) * r)
    if im is None:
        return (re * c, re * s)
    return (re * c - im * s, re * s + im * c)


def butterflies(z, sense):
    size = len(z)
    if size == 1:
        return z
    even = butterflies(z[0::2], sense)
    odd = butterflies(z[1::2], sense)
    odd = [turned(o, k, size, sense) for k, o in enumerate(odd)]
    head = [(plus(e[0], o[0]), plus(e[1], o[1])) for e, o in zip(even, odd)]
    tail = [(minus(e[0], o[0]), minus(e[1], o[1])) for e, o in zip(even, odd)]
    return head + tail


def twist(z, c, s, sense):
    re, im = z
    if im is None:
        return (re * c, re * s * (-sense))
    if sense > 0:
        return (re * c + im * s, im * c - re * s)
    return (re * c - im * s, im * c + re * s)


def stencil(shift_plane, height, dipole, halos, tc, want_omega, part, parts, earlier=()):
    rows, cols = height.shape
    block = min(64, rows // (tc * parts))
    steps = rows // (block * parts)
    ahead = part * steps
    chunk = min(128, cols)
    wide = min(1024, cols)
    groups = block // SUB
    count = 4 if want_omega else 3
    tall = block + 2 * SUB
    last = rows // SUB - 1

    def kernel(*refs):
        if want_omega:
            arrays, refs = (refs[:9], refs[9:])
            top, bottom, left, right, omega_ref, pad, slope = refs
        else:
            arrays, refs = (refs[:6], refs[6:])
            refs = refs[:4] + refs[4 + len(earlier) :]
            top, bottom, left, right, unit_ref, base_ref, pad, slope, bend = refs
        i = pl.program_id(0) + ahead
        for f in range(count):
            trio = arrays[:3] if f < 2 else arrays[3 * (f - 1) : 3 * f]
            take = (lambda r: r[f]) if f < 2 else (lambda r: r[...])
            cur, prev, nxt = trio
            pad[f, SUB : SUB + block, LANES : LANES + cols] = take(cur)
            pad[f, 0:SUB, LANES : LANES + cols] = jnp.where(i == 0, top[f], take(prev))
            pad[f, SUB + block :, LANES : LANES + cols] = jnp.where(
                i == steps * parts - 1, bottom[f], take(nxt)
            )
            pad[f, :, 0:LANES] = left[f, pl.ds(pl.multiple_of(i * block, SUB), tall), :]
            pad[f, :, LANES + cols :] = right[f, pl.ds(pl.multiple_of(i * block, SUB), tall), :]

        def along(g, carry):
            r = pl.ds(pl.multiple_of(g * SUB, SUB), SUB)
            for f in range(count):
                for j in range(cols // wide):
                    width = wide + 2 * LANES
                    x = pad[f, r, j * wide : j * wide + width]
                    roll = lambda k: pltpu.roll(x, k % width, 1)[:, LANES : LANES + wide]
                    m2, m1, p1, p2 = roll(2), roll(1), roll(-1), roll(-2)
                    here = slice(j * wide, (j + 1) * wide)
                    slope[f, r, here] = ((m2 - p2) + 8.0 * (p1 - m1)) * (1.0 / 12.0)
                    if not want_omega:
                        mid = x[:, LANES : LANES + wide]
                        bend[f, r, here] = (16.0 * (m1 + p1) - (m2 + p2) - 30.0 * mid) * (
                            1.0 / 12.0
                        )
            return carry

        lax.fori_loop(0, tall // SUB, along, 0)

        def across(j, carry):
            inner = pl.ds(pl.multiple_of(j * chunk, LANES), chunk)
            outer = pl.ds(pl.multiple_of(j * chunk + LANES, LANES), chunk)
            for g in range(groups):
                at = lambda ref, f, k, lanes: ref[f, SUB * (g + 1) + k : SUB * (g + 2) + k, lanes]

                def first(ref, f, lanes):
                    return (
                        (at(ref, f, -2, lanes) - at(ref, f, 2, lanes))
                        + 8.0 * (at(ref, f, 1, lanes) - at(ref, f, -1, lanes))
                    ) * (1.0 / 12.0)

                ga = [first(pad, f, outer) for f in range(count)]
                gb = [at(slope, f, 0, inner) for f in range(count)]
                ta = (1.0 + ga[0], ga[1], ga[2])
                tb = (gb[0], 1.0 + gb[1], gb[2])
                n = (
                    ta[1] * tb[2] - ta[2] * tb[1],
                    ta[2] * tb[0] - ta[0] * tb[2],
                    ta[0] * tb[1] - ta[1] * tb[0],
                )
                inv = 1.0 / jnp.sqrt(n[0] * n[0] + n[1] * n[1] + n[2] * n[2])
                out = slice(g * SUB, (g + 1) * SUB)
                if want_omega:
                    omega_ref[0, 0, out, inner] = ga[3] * inv
                    omega_ref[0, 1, out, inner] = gb[3] * inv
                    continue
                unit = [v * inv for v in n]
                for f in range(3):
                    unit_ref[f, out, inner] = unit[f]
                big_e = ta[0] * ta[0] + ta[1] * ta[1] + ta[2] * ta[2]
                big_f = ta[0] * tb[0] + ta[1] * tb[1] + ta[2] * tb[2]
                big_g = tb[0] * tb[0] + tb[1] * tb[1] + tb[2] * tb[2]
                sl = sm = sn = None
                for f in range(3):
                    mid = at(pad, f, 0, outer)
                    aa = (
                        16.0 * (at(pad, f, -1, outer) + at(pad, f, 1, outer))
                        - (at(pad, f, -2, outer) + at(pad, f, 2, outer))
                        - 30.0 * mid
                    ) * (1.0 / 12.0)
                    sl = plus(sl, aa * unit[f])
                    sm = plus(sm, first(slope, f, inner) * unit[f])
                    sn = plus(sn, at(bend, f, 0, inner) * unit[f])
                curvature = (big_e * sn - 2.0 * big_f * sm + big_g * sl) * (0.5 * inv * inv)
                base_ref[out, inner] = -0.5 * at(pad, 2, 0, outer) + 0.3 * curvature
            return carry

        lax.fori_loop(0, cols // chunk, across, 0)

    per = block // SUB
    plane = [
        pl.BlockSpec((block, cols), lambda i: (i + ahead, 0)),
        pl.BlockSpec((SUB, cols), lambda i: (jnp.maximum((i + ahead) * per - 1, 0), 0)),
        pl.BlockSpec((SUB, cols), lambda i: (jnp.minimum((i + ahead + 1) * per, last), 0)),
    ]
    pair = [
        pl.BlockSpec((2, block, cols), lambda i: (0, i + ahead, 0)),
        pl.BlockSpec((2, SUB, cols), lambda i: (0, jnp.maximum((i + ahead) * per - 1, 0), 0)),
        pl.BlockSpec(
            (2, SUB, cols), lambda i: (0, jnp.minimum((i + ahead + 1) * per, last), 0)
        ),
    ]
    whole = [pl.BlockSpec(h.shape, lambda i: (0, 0, 0)) for h in halos]
    ins = [shift_plane] * 3 + [height] * 3 + ([dipole] * 3 if want_omega else [])
    scratch = [
        pltpu.VMEM((count, tall, cols + 2 * LANES), jnp.float32),
        pltpu.VMEM((count, tall, cols), jnp.float32),
    ]
    f32 = lambda *dims: jax.ShapeDtypeStruct(dims, jnp.float32)
    if want_omega:
        half = steps // tc
        out_shape = f32(tc, 2, rows // (tc * parts), cols)
        out_specs = pl.BlockSpec((1, 2, block, cols), lambda i: (i // half, 0, i % half, 0))
    else:
        out_shape = (f32(3, rows, cols), f32(rows, cols))
        out_specs = (
            pl.BlockSpec((3, block, cols), lambda i: (0, i + ahead, 0)),
            pl.BlockSpec((block, cols), lambda i: (i + ahead, 0)),
        )
        scratch.append(pltpu.VMEM((count, tall, cols), jnp.float32))
    return pl.pallas_call(
        kernel,
        grid=(steps,),
        in_specs=pair + plane * (count - 2) + whole + [pl.BlockSpec(memory_space=pl.ANY)] * len(earlier),
        out_specs=out_specs,
        out_shape=out_shape,
        scratch_shapes=scratch,
        compiler_params=params(),
        input_output_aliases={len(ins) + 4 + k: k for k in range(len(earlier))},
        name="omega" if want_omega else "geometry",
    )(*ins, *halos, *earlier)


def row_tables(outer, inner, length):
    c, s = unit_circle(outer, inner, length)
    table = np.stack([c, s]).astype(np.float32)
    return jnp.broadcast_to(jnp.asarray(table)[:, :, None, :], (2, outer, SUB, inner))


def row_forward(omega, outer, inner):
    tc, _, rows, cols = omega.shape
    kept = inner // 2
    length = tc * cols
    block = min(64, rows)
    per = outer // tc
    c, s = unit_circle(inner, kept, inner)
    matrix = two_halves(np.block([[c, -s], [s, c]]))

    def kernel(x_ref, tw_ref, m_ref, out_ref, mid):
        def step(g, carry):
            r = pl.ds(pl.multiple_of(g * SUB, SUB), SUB)
            for j in range(0, inner, LANES):
                z = []
                for l in range(outer):
                    at = (l % per) * inner + j
                    z.append((x_ref[l // per, 0, r, at : at + LANES], None))
                z = butterflies(z, 1.0)
                for n in range(outer):
                    re, im = z[n]
                    if n:
                        re, im = twist(
                            z[n],
                            tw_ref[0, n, :, j : j + LANES],
                            tw_ref[1, n, :, j : j + LANES],
                            1.0,
                        )
                    if im is None:
                        im = jnp.zeros_like(re)
                    mid[n, r, j : j + LANES] = re
                    mid[n, r, inner + j : inner + j + LANES] = im
            return carry

        lax.fori_loop(0, block // SUB, step, 0)

        def finish(n, carry):
            y = product(split(mid[n]), (m_ref[0], m_ref[1]))
            out_ref[n, 0, 0] = y[:, :kept]
            out_ref[n, 1, 0] = y[:, kept:]
            return carry

        lax.fori_loop(0, outer, finish, 0, unroll=4)

    return pl.pallas_call(
        kernel,
        grid=(2, rows // block),
        in_specs=[
            pl.BlockSpec((tc, 1, block, cols), lambda p, i: (0, p, i, 0)),
            pl.BlockSpec((2, outer, SUB, inner), lambda p, i: (0, 0, 0, 0)),
            pl.BlockSpec(matrix.shape, lambda p, i: (0, 0, 0)),
        ],
        out_specs=pl.BlockSpec((outer, 2, 1, block, kept), lambda p, i: (0, 0, p, i, 0)),
        out_shape=jax.ShapeDtypeStruct((outer, 2, 2, rows, kept), jnp.float32),
        scratch_shapes=[pltpu.VMEM((outer, block, 2 * inner), jnp.float32)],
        compiler_params=params(),
        name="rows_forward",
    )(omega, row_tables(outer, inner, length), jnp.asarray(matrix))


def column_table(outer, inner, width):
    c, s = unit_circle(outer, inner, outer * inner)
    table = jnp.asarray(np.stack([c, s]).astype(np.float32))
    return jnp.broadcast_to(table[..., None], (2, outer, inner, width))


def column_middle(spectra, table, freq_two, live_two, outer, inner, tc):
    length = outer * inner
    pieces = len(spectra)
    short, width = spectra[0].shape[-2:]
    sub = inner // (short * tc)
    parts = pieces // sub
    c, s = unit_circle(inner, inner, inner)
    matrix = two_halves(np.concatenate([c, s], 0))

    def kernel(*refs):
        x_refs, refs = (refs[:pieces], refs[pieces:])
        tw_ref, m_ref, f_ref, live_ref = refs[:4]
        out_refs, mid = (refs[4:-1], refs[-1])

        for q in range(sub):

            def down(g, carry):
                r = pl.ds(pl.multiple_of(g * SUB + q * short * tc, SUB), SUB)
                core = g // (short // SUB)
                t = pl.ds(pl.multiple_of(g % (short // SUB) * SUB, SUB), SUB)
                for p in range(2):
                    z = []
                    for a in range(outer):
                        ref, peer = (x_refs[a % parts * sub + q], a // parts * tc + core)
                        z.append((ref[peer, 0, p, t, :], ref[peer, 1, p, t, :]))
                    z = butterflies(z, 1.0)
                    for k in range(outer):
                        v = z[k]
                        if k:
                            v = twist(v, tw_ref[0, k, r], tw_ref[1, k, r], 1.0)
                        mid[k, r, (2 * p) * width : (2 * p + 1) * width] = v[0]
                        mid[k, r, (2 * p + 1) * width : (2 * p + 2) * width] = v[1]
                return carry

            lax.fori_loop(0, short * tc // SUB, down, 0)

        fre_two = f_ref[...]
        live_cols = live_ref[...]
        weights = (m_ref[0], m_ref[1])

        def turn(k, carry):
            y = product(weights, split(mid[k]))
            parts = []
            for p in range(2):
                lo = slice((2 * p) * width, (2 * p + 1) * width)
                hi = slice((2 * p + 1) * width, (2 * p + 2) * width)
                parts.append((y[:inner, lo] + y[inner:, hi], y[:inner, hi] - y[inner:, lo]))
            number = k + outer * lax.broadcasted_iota(jnp.int32, (inner, width), 0)
            signed = jnp.where(number >= length // 2, number - length, number)
            fre_one = signed.astype(jnp.float32) * (1.0 / length)
            radius = jnp.sqrt(fre_one * fre_one + fre_two * fre_two)
            live = (number != length // 2) & (live_cols > 0.0) & (radius > 0.0)
            factor = jnp.where(live, 0.5 / jnp.where(live, radius, 1.0), 0.0)
            one = factor * fre_one
            two = factor * fre_two
            sum_re = one * parts[0][0] + two * parts[1][0]
            sum_im = one * parts[0][1] + two * parts[1][1]
            w = jnp.concatenate([sum_im, -sum_re], 1)
            y = product(weights, split(w))
            mid[k, :, :width] = y[:inner, :width] - y[inner:, width:]
            mid[k, :, width : 2 * width] = y[:inner, width:] + y[inner:, :width]
            return carry

        lax.fori_loop(0, outer, turn, 0)

        for h, out_ref in enumerate(out_refs):

            def up(g, carry):
                r = pl.ds(pl.multiple_of(g * SUB + h * length // outer // parts, SUB), SUB)
                t = pl.ds(pl.multiple_of(g * SUB, SUB), SUB)
                z = []
                for k in range(outer):
                    v = (mid[k, r, :width], mid[k, r, width : 2 * width])
                    z.append(v if k == 0 else twist(v, tw_ref[0, k, r], tw_ref[1, k, r], -1.0))
                z = butterflies(z, -1.0)
                for a in range(outer):
                    out_ref[a, 0, t, :] = z[a][0] * (1.0 / length)
                    out_ref[a, 1, t, :] = z[a][1] * (1.0 / length)
                return carry

            lax.fori_loop(0, inner // parts // SUB, up, 0)

    return pl.pallas_call(
        kernel,
        out_shape=[jax.ShapeDtypeStruct((outer, 2, inner // parts, width), jnp.float32)] * parts,
        scratch_shapes=[pltpu.VMEM((outer, inner, 4 * width), jnp.float32)],
        compiler_params=params(),
        name="columns",
    )(*spectra, table, jnp.asarray(matrix), freq_two, live_two)


def row_inverse(partial, outer, inner, tc):
    _, _, rows, kept = partial.shape
    length = outer * inner
    cols = length // tc
    per = outer // tc
    block = min(64, rows)
    c, s = unit_circle(kept, inner, inner)
    matrix = two_halves(np.block([[c, s], [-s, c]]) * (2.0 / length))

    def kernel(x_ref, tw_ref, m_ref, out_ref, mid):
        lane = lax.broadcasted_iota(jnp.int32, (block, kept), 1)

        def start(n, carry):
            weight = jnp.where((lane == 0) & (n == 0), 0.5, 1.0)
            w = jnp.concatenate([x_ref[n, 0] * weight, x_ref[n, 1] * weight], 1)
            mid[n] = product(split(w), (m_ref[0], m_ref[1]))
            return carry

        lax.fori_loop(0, outer, start, 0, unroll=4)

        def step(g, carry):
            r = pl.ds(pl.multiple_of(g * SUB, SUB), SUB)
            for j in range(0, inner, LANES):
                z = []
                for n in range(outer):
                    v = (mid[n, r, j : j + LANES], mid[n, r, inner + j : inner + j + LANES])
                    if n:
                        v = twist(
                            v,
                            tw_ref[0, n, :, j : j + LANES],
                            tw_ref[1, n, :, j : j + LANES],
                            -1.0,
                        )
                    z.append(v)
                z = butterflies(z, -1.0)
                for l in range(outer):
                    at = (l % per) * inner + j
                    out_ref[l // per, r, at : at + LANES] = z[l][0]
            return carry

        lax.fori_loop(0, block // SUB, step, 0)

    return pl.pallas_call(
        kernel,
        grid=(rows // block,),
        in_specs=[
            pl.BlockSpec((outer, 2, block, kept), lambda i: (0, 0, i, 0)),
            pl.BlockSpec((2, outer, SUB, inner), lambda i: (0, 0, 0, 0)),
            pl.BlockSpec(matrix.shape, lambda i: (0, 0, 0)),
        ],
        out_specs=pl.BlockSpec((tc, block, cols), lambda i: (0, i, 0)),
        out_shape=jax.ShapeDtypeStruct((tc, rows, cols), jnp.float32),
        scratch_shapes=[pltpu.VMEM((outer, block, 2 * inner), jnp.float32)],
        compiler_params=params(),
        name="rows_inverse",
    )(partial, row_tables(outer, inner, length), jnp.asarray(matrix))


def ring(axis):
    devices = lax.axis_size(axis)
    up = [(i, (i + 1) % devices) for i in range(devices)]
    return up, [(j, i) for i, j in up]


def edges(shift_plane, height, dipole):
    fields = lambda cut: jnp.concatenate([cut(shift_plane), cut(height[None]), cut(dipole[None])], 0)
    up, down = ring("tr")
    top = lax.ppermute(fields(lambda x: x[:, -SUB:]), "tr", up)
    bottom = lax.ppermute(fields(lambda x: x[:, :SUB]), "tr", down)

    def slab(lanes):
        body = fields(lambda x: x[..., lanes])
        return jnp.concatenate([top[..., lanes], body, bottom[..., lanes]], 1)

    up, down = ring("tc")
    left = lax.ppermute(slab(slice(-LANES, None)), "tc", up)
    right = lax.ppermute(slab(slice(0, LANES)), "tc", down)
    return top, bottom, left, right


def exchange(x):
    other = 1 - lax.axis_index("tc")
    sent = lax.dynamic_index_in_dim(x, other, 0, keepdims=True)
    got = lax.ppermute(sent, "tc", ring("tc")[0])
    return lax.dynamic_update_slice_in_dim(x, got, other, 0)


def local_kernels(shift_plane, height, dipole):
    tc = lax.axis_size("tc")
    rows, cols = height.shape
    col_outer, col_inner = factors(cols * tc)
    row_outer, row_inner = factors(rows * lax.axis_size("tr"))
    kept = col_inner // 2
    halos = edges(shift_plane, height, dipole)
    parts = rows // row_inner
    pieces = 2 * parts
    spectra = []
    charge = dipole
    for part in range(pieces):
        omega = stencil(shift_plane, height, charge, halos, tc, True, part, pieces)
        omega = exchange(omega)
        block = row_forward(omega, col_outer, col_inner)
        block, charge = lax.optimization_barrier((block, dipole))
        block = lax.all_to_all(block, ("tr", "tc"), split_axis=0, concat_axis=0, tiled=True)
        spectra.append(block)
    planes = stencil(shift_plane, height, dipole, halos, tc, False, 0, parts)
    place = lax.axis_index(("tr", "tc")) * kept + jnp.arange(kept, dtype=jnp.int32)
    freq_two, nyquist_two = wavenumbers(cols * tc, kept, place)
    live_two = jnp.where(nyquist_two, 0.0, 1.0)
    table = column_table(row_outer, row_inner, kept)
    spectra, planes, table = lax.optimization_barrier((spectra, planes, table))
    partial = column_middle(
        spectra, table, freq_two[None, :], live_two[None, :], row_outer, row_inner, tc
    )
    for part in range(1, parts):
        planes = stencil(shift_plane, height, dipole, halos, tc, False, part, parts, planes)
    unit, base = planes
    results = ()
    for part in range(parts):
        block = lax.all_to_all(partial[part], ("tr", "tc"), split_axis=0, concat_axis=0, tiled=True)
        speed = row_inverse(block, col_outer, col_inner, tc)
        speed = exchange(speed)
        results = finish(speed, unit, base, part, parts, results)
    return tuple(results)


def finish(speed, unit, base, part, parts, earlier):
    _, cols = base.shape
    tc, short, _ = speed.shape
    block = min(64, short)
    steps = short // block

    def kernel(s_ref, u_ref, b_ref, *refs):
        v_ref, d_ref = refs[len(earlier) :]
        s = s_ref[0]
        for f in range(3):
            v_ref[f] = s * u_ref[f]
        d_ref[...] = b_ref[...] + 0.5 * s * s

    row = lambda t, j: (t * parts + part) * steps + j
    plane = pl.BlockSpec((block, cols), lambda t, j: (row(t, j), 0))
    triple = pl.BlockSpec((3, block, cols), lambda t, j: (0, row(t, j), 0))
    return pl.pallas_call(
        kernel,
        grid=(tc, steps),
        in_specs=[pl.BlockSpec((1, block, cols), lambda t, j: (t, j, 0)), triple, plane]
        + [pl.BlockSpec(memory_space=pl.ANY)] * len(earlier),
        out_specs=(triple, plane),
        out_shape=(
            jax.ShapeDtypeStruct(unit.shape, jnp.float32),
            jax.ShapeDtypeStruct(base.shape, jnp.float32),
        ),
        input_output_aliases={3 + k: k for k in range(len(earlier))},
        compiler_params=params(),
        name="finish",
    )(speed, unit, base, *earlier)


def fits(rows, cols, tr, tc):
    col_outer, col_inner = factors(cols * tc)
    row_outer, row_inner = factors(rows * tr)
    peers = tr * tc
    return (
        tc == 2
        and col_outer == row_outer == peers == 16
        and col_inner // 2 == LANES
        and rows // tc == row_inner
        and rows % (tc * tc * SUB) == 0
        and rows % (SUB * tc) == 0
        and col_outer % tc == 0
    )


def solution(mesh):
    in_specs = (
        P(None, ("groups", "tr"), "tc"),
        P(("groups", "tr"), "tc"),
        P(("groups", "tr"), "tc"),
    )
    out_specs = (P(None, ("groups", "tr"), "tc"), P(("groups", "tr"), "tc"))

    def chosen(shift_plane, height, dipole):
        rows, cols = height.shape
        if fits(rows, cols, lax.axis_size("tr"), lax.axis_size("tc")):
            return local_kernels(shift_plane, height, dipole)
        return local(shift_plane, height, dipole)

    return jax.shard_map(
        chosen, mesh=mesh, in_specs=in_specs, out_specs=out_specs, check_vma=False
    )
```
